32 devices in a mesh: dp: 8 (over z, y), tensor: 4 (over x, core).
Axes of the slice: x: 2, y: 2, z: 4, core: 2. Of those that a mesh axis runs over, the one named last changes fastest.
Arguments:
- tokens: bfloat16 [8192, 512], P('dp'), may hold values from -6 to 6
- cotangent: bfloat16 [8192, 512], P('dp'), may hold values from -6 to 6
- w_query: float32 [512, 512], P('dp', 'tensor'), may hold values from -0.125 to 0.125
- w_key: float32 [512, 512], P('dp', 'tensor'), may hold values from -0.125 to 0.125
- w_value: float32 [512, 512], P('dp', 'tensor'), may hold values from -0.25 to 0.25
- w_out: float32 [512, 512], P('tensor', 'dp'), may hold values from -1 to 1
- w_gate: float32 [512, 2048], P('dp', 'tensor'), may hold values from -0.25 to 0.25
- w_up: float32 [512, 2048], P('dp', 'tensor'), may hold values from -0.25 to 0.25
- w_down: float32 [2048, 512], P('tensor', 'dp'), may hold values from -0.125 to 0.125
- norm_attn: float32 [512], P('dp'), may hold values from 0.5 to 1.5
- norm_ffn: float32 [512], P('dp'), may hold values from 0.5 to 1.5
- bias_table: float32 [32, 8], P('dp', 'tensor'), may hold values from -5 to 5
- buckets: int32 [1024, 1024], replicated, may hold values from 0 to 31
- padding: int32 [8, 1024], P('dp'), may hold values from 0 to 1, as said below
Outputs:
- block_out: bfloat16 [8192, 512], P('dp')
- input_grad: float32 [8192, 512], P('dp')
- grad_query: float32 [512, 512], P('dp', 'tensor')
- grad_key: float32 [512, 512], P('dp', 'tensor')
- grad_value: float32 [512, 512], P('dp', 'tensor')
- grad_out: float32 [512, 512], P('tensor', 'dp')
- grad_gate: float32 [512, 2048], P('dp', 'tensor')
- grad_up: float32 [512, 2048], P('dp', 'tensor')
- grad_down: float32 [2048, 512], P('tensor', 'dp')
- grad_norm_attn: float32 [512], P('dp')
- grad_norm_ffn: float32 [512], P('dp')
- grad_bias: float32 [32, 8], P('dp', 'tensor')
The draws below stay inside these ranges and needn't reach their ends.
Inputs may be any that keep to these rules, and one draw needn't show every extreme that they name: Each row of padding is 1 on a leading run of positions, at least half of them, and 0 after it.
All inputs are finite; a program needn't handle non-finite values.
Results may differ from the reference program's by a relative error of at most 0.02.
Values may be sent and summed in bfloat16 or wider, within the bound.
A program may use at most 128 MiB of HBM per device.

```python
import math
import jax
import jax.numpy as jnp
from jax import lax

D = 512
HEADS = 8
HEAD_DIM = 64
FF = 2048
BUCKETS = 32
LENGTH = 1024
INNER = 512
SEQS = 8
TOKENS = 8192


def draw_padding(key, part):
    lengths = jax.random.randint(key, (SEQS, 1), LENGTH // 2, LENGTH + 1)
    positions = jnp.arange(LENGTH, dtype=jnp.int32)[None, :]
    return (positions < lengths).astype(jnp.int32)


def place_ends(values, own_key, smallest, largest):
    spot = [jax.random.randint(jax.random.fold_in(own_key, axis), (), 0, length) for axis, length in enumerate(values.shape)]
    widest = values.shape.index(max(values.shape))
    beside = spot[:widest] + [(spot[widest] + 1) % values.shape[widest]] + spot[widest + 1:]
    return values.at[tuple(spot)].set(smallest).at[tuple(beside)].set(largest)


def spiked(values, own_key, source, target, shards_of, factor):
    owner, partner = [(jnp.arange(values.shape[dim]) // (values.shape[dim] // shards_of)).reshape([-1 if axis == dim else 1 for axis in range(values.ndim)]) for dim in (source, target)]
    chosen = jax.random.permutation(own_key, shards_of)[partner]
    strong = (owner == chosen) | (owner == (partner + shards_of // 2) % shards_of)
    return jnp.where(strong, factor * values, values)


def block_scale(rng, dims, split, least, top_value):
    gain = 1.0
    for axis_at, shards_of in split:
        steps = jax.random.uniform(jax.random.fold_in(jax.random.fold_in(rng, 6), axis_at), (shards_of,), jnp.float32, least / len(split), top_value / len(split))
        gain = gain * jnp.repeat(jnp.exp(steps), dims[axis_at] // shards_of).reshape((-1,) + (1,) * (len(dims) - 1 - axis_at))
    return gain


def scatter_about(own_key, dims, width, bound, split=(), held_as=jnp.bfloat16):
    values = jax.random.normal(own_key, dims, jnp.float32) * width
    if len(split) > 0:
        values = block_scale(own_key, dims, split, -0.22, 0.18) * values
    return jnp.clip(values, min=-bound, max=bound).astype(held_as)


def bell_draw_with(key, shape, scale, most, pieces, heavy, held_as=jnp.bfloat16):
    array = scale * jax.random.normal(key, shape, jnp.float32)
    if pieces:
        array = array * block_scale(key, shape, pieces, -0.22, 0.18)
    return jnp.clip(spiked(array, jax.random.fold_in(key, 3), *heavy), -most, most).astype(held_as)


def setup_inputs(seed: int = 0) -> dict:
    keys = jax.random.split(jax.random.key(seed), 15)
    return {
        "tokens": bell_draw_with(keys[0], (TOKENS, D), 1.0, 6.0, ((0, 8),), (0, 1, 8, 2.0)),
        "cotangent": bell_draw_with(keys[1], (TOKENS, D), 1.0, 6.0, ((0, 8),), (0, 1, 8, 2.0)),
        "w_query": scatter_about(keys[2], (D, INNER), (4 * D) ** -0.5, 0.125, ((0, 8), (1, 4)), jnp.float32),
        "w_key": scatter_about(keys[3], (D, INNER), (4 * D) ** -0.5, 0.125, ((0, 8), (1, 4)), jnp.float32),
        "w_value": scatter_about(keys[4], (D, INNER), D ** -0.5, 0.25, ((0, 8), (1, 4)), jnp.float32),
        "w_out": scatter_about(keys[5], (INNER, D), (HEAD_DIM // 2) ** -0.5, 1.0, ((0, 4), (1, 8)), jnp.float32),
        "w_gate": scatter_about(keys[6], (D, FF), D ** -0.5, 0.25, ((0, 8), (1, 4)), jnp.float32),
        "w_up": scatter_about(keys[7], (D, FF), D ** -0.5, 0.25, ((0, 8), (1, 4)), jnp.float32),
        "w_down": scatter_about(keys[8], (FF, D), FF ** -0.5, 0.125, ((0, 4), (1, 8)), jnp.float32),
        "norm_attn": jnp.clip(1.0 + 0.1 * jax.random.normal(keys[9], (D,), jnp.float32), 0.5, 1.5),
        "norm_ffn": jnp.clip(1.0 + 0.1 * jax.random.normal(keys[10], (D,), jnp.float32), 0.5, 1.5),
        "bias_table": scatter_about(keys[11], (BUCKETS, HEADS), 1.0, 5.0, ((0, 8), (1, 4)), jnp.float32),
        "buckets": place_ends(jax.random.randint(keys[12], (LENGTH, LENGTH), 0, BUCKETS), jax.random.fold_in(keys[12], 1), 0, BUCKETS - 1).astype(jnp.int32),
        "padding": draw_padding(jax.random.fold_in(keys[14], 71), 0),
    }


epsilon = 1e-06
highest = lax.Precision.HIGHEST
masked_score = -1000000000.0

@jax.custom_vjp
def low(v):
    return lax.optimization_barrier(v.astype(jnp.bfloat16)).astype(jnp.float32)

@jax.custom_vjp
def low_back(v):
    return v

def low_keep(v):
    return (low(v), None)

def low_pass(kept, grad):
    return (grad,)

def back_keep(v):
    return (v, None)

def back_low(kept, grad):
    return (low(grad),)
low.defvjp(low_keep, low_pass)
low_back.defvjp(back_keep, back_low)

def rms_scale(values, scaling):
    return values * lax.rsqrt(lax.optimization_barrier(jnp.mean(values * values, axis=-1, keepdims=True)) + epsilon) * scaling

def attend_one(queries, keys_in, values, bias_heads, padding_row):
    scores = jnp.einsum('qhd,khd->hqk', queries, keys_in, precision=highest) + bias_heads
    scores = low_back(scores)
    scores = jnp.where(padding_row[None, None, :] > 0, scores, masked_score)
    row_max = lax.optimization_barrier(jnp.max(scores, axis=-1, keepdims=True))
    exponent = jnp.exp(scores - row_max)
    attention = exponent / lax.optimization_barrier(jnp.sum(exponent, axis=-1, keepdims=True))
    return jnp.einsum('hqk,khd->qhd', low(attention), values, precision=highest)

def layer_forward(block_in, w_query, w_key, w_value, w_out, w_gate, w_up, w_down, norm_attn, norm_ffn, bias_table, buckets, padding_group):
    group_size = block_in.shape[0]
    normed_attn = low(rms_scale(block_in, low(norm_attn)))

    def project(weight_master):
        product = jnp.einsum('gld,de->gle', normed_attn, low(weight_master), precision=highest)
        return low_back(low(product)).reshape(group_size, LENGTH, HEADS, HEAD_DIM)
    queries = project(w_query)
    keys_in = project(w_key)
    values = project(w_value)
    bias_heads = jnp.transpose(low(bias_table)[buckets], (2, 0, 1))
    attend_saved = jax.checkpoint(attend_one)

    def one_sequence(items):
        return attend_saved(items[0], items[1], items[2], bias_heads, items[3])
    head_mix = lax.map(one_sequence, (queries, keys_in, values, padding_group))
    head_mix = low_back(low(head_mix.reshape(group_size, LENGTH, INNER)))
    attn_out = low_back(jnp.einsum('gle,ed->gld', head_mix, low(w_out), precision=highest))
    middle = block_in + attn_out
    normed_ffn = low(rms_scale(middle, low(norm_ffn)))
    gate_proj = low_back(jnp.einsum('gld,df->glf', normed_ffn, low(w_gate), precision=highest))
    up_proj = low_back(jnp.einsum('gld,df->glf', normed_ffn, low(w_up), precision=highest))
    hidden = low(jax.nn.gelu(gate_proj, approximate=True) * up_proj)
    ffn_out = low_back(jnp.einsum('glf,fd->gld', hidden, low(w_down), precision=highest))
    return middle + ffn_out

def reference(tokens, cotangent, w_query, w_key, w_value, w_out, w_gate, w_up, w_down, norm_attn, norm_ffn, bias_table, buckets, padding):
    group_size = math.gcd(SEQS, max(1, 4096 // LENGTH))
    group_count = SEQS // group_size
    inputs = tokens.astype(jnp.float32).reshape(group_count, group_size, LENGTH, D)
    grads_in = cotangent.astype(jnp.float32).reshape(group_count, group_size, LENGTH, D)
    paddings = padding.reshape(group_count, group_size, LENGTH)
    weights = (w_query, w_key, w_value, w_out, w_gate, w_up, w_down, norm_attn, norm_ffn, bias_table)

    def scan_step(totals, items):
        block_in, grad_group, padding_group = items

        def forward(inner_in, wq_in, wk_in, wv_in, wo_in, wg_in, wu_in, wd_in, ga_in, gf_in, table_in):
            return layer_forward(inner_in, wq_in, wk_in, wv_in, wo_in, wg_in, wu_in, wd_in, ga_in, gf_in, table_in, buckets, padding_group)
        outputs, pullback = jax.vjp(forward, block_in, *weights)
        grads = pullback(grad_group)
        totals = tuple((former + latter for former, latter in zip(totals, grads[1:])))
        return (totals, (outputs, grads[0]))
    zeros_start = tuple((jnp.zeros_like(weight_master) for weight_master in weights))
    totals, (outputs, input_grads) = lax.scan(scan_step, zeros_start, (inputs, grads_in, paddings))
    return (outputs.reshape(TOKENS, D).astype(jnp.bfloat16), input_grads.reshape(TOKENS, D), totals[0], totals[1], totals[2], totals[3], totals[4], totals[5], totals[6], totals[7], totals[8], totals[9])
```

```python
import functools

import jax
import jax.numpy as jnp
from jax import lax
from jax.experimental import pallas as pl
from jax.experimental.pallas import tpu as pltpu
from jax.sharding import PartitionSpec as P

MESH = pl.DeviceIdType.MESH
BF = jnp.bfloat16
F32 = jnp.float32
NN = (((1,), (0,)), ((), ()))
NT = (((1,), (1,)), ((), ()))
TN = (((0,), (0,)), ((), ()))
epsilon = 1e-06
masked_score = -1000000000.0
LANES = 128
BUCKETS = 32


def dot(former, latter, dims):
    return lax.dot_general(former, latter, dims, preferred_element_type=F32)


def rows_of(index, size):
    return pl.ds(pl.multiple_of(index * size, size), size)


def lookup(table, ids):
    tiles = ids.shape[1] // LANES
    return jnp.concatenate(
        [
            jnp.take_along_axis(table, ids[:, c * LANES : (c + 1) * LANES], axis=1)
            for c in range(tiles)
        ],
        axis=1,
    )


class Comm:
    def __init__(self, sizes, sems):
        self.Z, self.Y, self.X = sizes
        self.sems = sems
        self.used = 0
        self.d, self.t = lax.axis_index("dp"), lax.axis_index("tensor")
        self.z, self.y = self.d // self.Y, self.d % self.Y
        self.x, self.c = self.t // 2, self.t % 2
        self.pending = []

    def z_peer(self, k):
        return ((self.z + k) % self.Z) * self.Y + self.y, self.t

    def y_peer(self, j):
        return self.z * self.Y + (self.y + j) % self.Y, self.t

    def x_peer(self, j):
        return self.d, ((self.x + j) % self.X) * 2 + self.c

    def core_peer(self):
        return self.d, self.x * 2 + (1 - self.c)

    def origin(self, kz, j=0):
        return ((self.z - kz) % self.Z) * self.Y + (self.y - j) % self.Y

    def pair(self):
        self.used += 2
        return self.sems.at[self.used - 2], self.sems.at[self.used - 1]

    def barrier(self):
        peers = [self.z_peer(k) for k in range(1, self.Z)]
        peers += [self.y_peer(j) for j in range(1, self.Y)]
        peers += [self.x_peer(j) for j in range(1, self.X)]
        peers += [self.core_peer()]
        semaphore = pltpu.get_barrier_semaphore()
        for peer in peers:
            pl.semaphore_signal(semaphore, inc=1, device_id=peer, device_id_type=MESH)
        pl.semaphore_wait(semaphore, len(peers))

    def copy(self, src, dst, peer, pair):
        return pltpu.make_async_remote_copy(
            src_ref=src,
            dst_ref=dst,
            send_sem=pair[0],
            recv_sem=pair[1],
            device_id=peer,
            device_id_type=MESH,
        )

    def send(self, src, dst, peer, pair):
        made = self.copy(src, dst, peer, pair)
        made.start()
        self.pending.append(made)

    def drain(self):
        for made in self.pending:
            made.wait_send()
        self.pending = []


class Gather:
    def __init__(self, comm, full):
        self.comm, self.full = comm, full
        Z, Y = comm.Z, comm.Y
        self.zp = {k: comm.pair() for k in range(1, Z)}
        self.yp = {(k, j): comm.pair() for k in range(Z) for j in range(1, Y)}

    def send_y(self, k):
        m = self.comm
        block = self.full.at[m.origin(k)]
        for j in range(1, m.Y):
            m.send(block, block, m.y_peer(j), self.yp[k, j])

    def start(self):
        m = self.comm
        own = self.full.at[m.d]
        for k in range(m.Z - 1, 0, -1):
            m.send(own, own, m.z_peer(k), self.zp[k])
        self.send_y(0)

    def forward(self):
        m = self.comm
        for k in range(1, m.Z):
            block = self.full.at[m.origin(k)]
            m.copy(block, block, m.z_peer(k), self.zp[k]).wait_recv()
            self.send_y(k)

    def finish(self):
        m = self.comm
        for k in range(m.Z):
            for j in range(1, m.Y):
                block = self.full.at[m.origin(k, j)]
                m.copy(block, block, m.y_peer(j), self.yp[k, j]).wait_recv()


def first_kernel(
    sizes,
    heads,
    x_hbm,
    wq_hbm,
    wk_hbm,
    wv_hbm,
    wo_hbm,
    wg_hbm,
    wu_hbm,
    wd_hbm,
    ga_hbm,
    gf_hbm,
    bt_hbm,
    bucket_hbm,
    pad_hbm,
    wa_out,
    wo_out,
    wg_out,
    wu_out,
    wd_out,
    misc_out,
    n1_out,
    q_out,
    k_out,
    v_out,
    p_out,
    o_out,
    x_v,
    sa,
    so,
    sg,
    su,
    sd,
    sga,
    sgf,
    sbt,
    bucket_v,
    pad_v,
    wa,
    wo,
    wg,
    wu,
    wd,
    misc,
    n1_v,
    q_v,
    k_v,
    v_v,
    p_v,
    o_v,
    local_sems,
    out_sems,
    sems,
):
    T, D = x_v.shape
    dp, R, I3 = wa.shape
    BR, _ = bt_hbm.shape
    I = wo.shape[2]
    HD = I // heads
    loads = [
        (wq_hbm, sa.at[0]),
        (wk_hbm, sa.at[1]),
        (wv_hbm, sa.at[2]),
        (ga_hbm, sga),
        (gf_hbm, sgf),
        (bt_hbm, sbt),
        (wo_hbm, so),
        (wg_hbm, sg),
        (wu_hbm, su),
        (wd_hbm, sd),
        (x_hbm, x_v),
        (bucket_hbm, bucket_v),
        (pad_hbm, pad_v),
    ]
    loads = [pltpu.make_async_copy(a, b, local_sems.at[n]) for n, (a, b) in enumerate(loads)]
    for load in loads:
        load.start()
    comm = Comm(sizes, sems)
    comm.barrier()
    g_misc, g_a, g_o, g_g, g_u, g_d = [Gather(comm, f) for f in (misc, wa, wo, wg, wu, wd)]
    d = comm.d
    for load in loads[:6]:
        load.wait()
    for n in range(3):
        wa[d, :, n * I : (n + 1) * I] = sa[n].astype(BF)
    misc[d] = jnp.zeros(misc.shape[1:], F32)
    misc[d, 0:1, 0:R] = sga[...]
    misc[d, 1:2, 0:R] = sgf[...]
    misc[d, 2 : 2 + BR, 0:heads] = sbt[...]
    g_a.start()
    g_misc.start()
    loads[6].wait()
    wo[d] = so[...].T.astype(BF)
    g_o.start()
    loads[7].wait()
    wg[d] = sg[...].astype(BF)
    g_g.start()
    loads[8].wait()
    wu[d] = su[...].astype(BF)
    g_u.start()
    loads[9].wait()
    wd[d] = sd[...].T.astype(BF)
    g_d.start()
    for load in loads[10:]:
        load.wait()
    g_a.forward()
    g_misc.forward()
    g_a.finish()
    g_misc.finish()
    gain = jnp.concatenate([misc[n, 0:1, 0:R] for n in range(dp)], axis=1)
    gain = gain.astype(BF).astype(F32)
    flat = misc[...].reshape(dp * 8, LANES).astype(BF)
    row = lax.broadcasted_iota(jnp.int32, flat.shape, 0)
    lane = lax.broadcasted_iota(jnp.int32, flat.shape, 1)
    chosen = (row // 8 == lane // BR) & (row % 8 - 2 == lane % BR) & (lane < BUCKETS)
    table = dot(flat, jnp.where(chosen, 1.0, 0.0).astype(BF), TN)[0:8]
    block = 256

    def project(i, carry):
        rows = rows_of(i, block)
        x = x_v[rows, :].astype(F32)
        r = lax.rsqrt(jnp.mean(x * x, axis=1, keepdims=True) + epsilon)
        n1 = (x * r * gain).astype(BF)
        n1_v[rows, :] = n1
        made = dot(n1, wa[...].reshape(D, I3), NN).astype(BF)
        for h in range(heads):
            for n, ref in enumerate((q_v, k_v, v_v)):
                ref[h, rows, :] = made[:, n * I + h * HD : n * I + (h + 1) * HD]
        return carry

    lax.fori_loop(0, T // block, project, 0)
    g_o.forward()
    g_g.forward()
    real = pad_v[...] > 0
    sub = 128

    def attend(i, carry):
        rows = rows_of(i, sub)
        ids = bucket_v[rows, :]
        for h in range(heads):
            scores = dot(q_v[h, rows, :], k_v[h], NT)
            bias = lookup(jnp.broadcast_to(table[h : h + 1, :], (sub, LANES)), ids)
            scores = jnp.where(real, scores + bias, masked_score)
            top = jnp.max(scores, axis=1, keepdims=True)
            e = jnp.exp(scores - top)
            inverse = 1.0 / jnp.sum(e, axis=1, keepdims=True)
            p = (e * inverse).astype(BF)
            p_v[h, rows, :] = p
            o_v[h, rows, :] = dot(p, v_v[h], NN)
        return carry

    lax.fori_loop(0, T // sub, attend, 0)
    g_u.forward()
    g_d.forward()
    for g in (g_o, g_g, g_u, g_d):
        g.finish()
    comm.drain()
    stores = [
        (wa, wa_out),
        (wo, wo_out),
        (wg, wg_out),
        (wu, wu_out),
        (wd, wd_out),
        (misc, misc_out),
        (n1_v, n1_out),
        (q_v, q_out),
        (k_v, k_out),
        (v_v, v_out),
        (p_v, p_out),
        (o_v, o_out),
    ]
    stores = [pltpu.make_async_copy(a, b, out_sems.at[n]) for n, (a, b) in enumerate(stores)]
    for store in stores:
        store.start()
    for store in stores:
        store.wait()


def back_kernel(heads, q_v, k_v, v_v, do_v, o_v, p_v, bucket_v, dq_o, dk_o, dv_o, bg_o, ds_v):
    T = q_v.shape[1]
    G = 32
    sub = 128
    bg_o[...] = jnp.zeros_like(bg_o)

    def body(i, carry):
        rows = rows_of(i, sub)
        kept = []
        for h in range(heads):
            do = do_v[h, rows, :]
            delta = jnp.sum(do.astype(F32) * o_v[h, rows, :], axis=1, keepdims=True)
            dp = dot(do, v_v[h], NT)
            ds = (p_v[h, rows, :].astype(F32) * (dp - delta)).astype(BF)
            ds_v[h, rows, :] = ds
            kept.append(ds)
            dq_o[h, rows, :] = dot(ds, k_v[h], NN).astype(BF)
        ids = bucket_v[rows, :]
        high = (ids >> 2).astype(BF)
        low = (ids & 3).astype(BF)
        for g in range(sub // G):
            part = slice(g * G, (g + 1) * G)
            hi, lo = high[part], low[part]
            one, zero = jnp.ones_like(hi), jnp.zeros_like(hi)
            left = jnp.concatenate(
                [jnp.where(hi == BF(b), one, zero) for b in range(BUCKETS // 4)], axis=0
            )
            right = []
            for b in range(4):
                match = lo == BF(b)
                right += [jnp.where(match, ds[part], zero) for ds in kept]
            bg_o[...] += dot(left, jnp.concatenate(right, axis=0), NT)
        return carry

    lax.fori_loop(0, T // sub, body, 0)
    for h in range(heads):
        dk_o[h] = dot(ds_v[h], q_v[h], TN).astype(BF)
        dv_o[h] = dot(p_v[h], do_v[h], TN).astype(BF)
    left = lax.broadcasted_iota(jnp.int32, bg_o.shape, 0)
    right = lax.broadcasted_iota(jnp.int32, bg_o.shape, 1)
    bg_o[...] = jnp.where(left % G == right % G, bg_o[...], 0.0)


def rms_scale(values, scaling):
    return values * lax.rsqrt(jnp.mean(values * values, axis=-1, keepdims=True) + epsilon) * scaling


def gated_unit(gate_proj, up_proj):
    return jax.nn.gelu(gate_proj, approximate=True) * up_proj


def per_device(
    sizes,
    tokens,
    cotangent,
    w_query,
    w_key,
    w_value,
    w_out,
    w_gate,
    w_up,
    w_down,
    norm_attn,
    norm_ffn,
    bias_table,
    buckets,
    padding,
):
    T, D = tokens.shape
    R, I = w_query.shape
    F = w_gate.shape[1]
    BR, heads = bias_table.shape
    HD = I // heads
    Z, Y, X = sizes
    dp = Z * Y
    S = jax.ShapeDtypeStruct
    V = pltpu.VMEM
    shapes = [
        S((dp, R, 3 * I), BF),
        S((dp, R, I), BF),
        S((dp, R, F), BF),
        S((dp, R, F), BF),
        S((dp, R, F), BF),
        S((dp, 8, LANES), F32),
        S((T, D), BF),
        S((heads, T, HD), BF),
        S((heads, T, HD), BF),
        S((heads, T, HD), BF),
        S((heads, T, T), BF),
        S((heads, T, HD), F32),
    ]
    wa, wo, wg, wu, wd, misc, normed_low, q, k, v, p, o = pl.pallas_call(
        functools.partial(first_kernel, sizes, heads),
        out_shape=shapes,
        in_specs=[pl.BlockSpec(memory_space=pl.ANY)] * 13,
        out_specs=[pl.BlockSpec(memory_space=pl.ANY)] * len(shapes),
        scratch_shapes=[
            V((T, D), BF),
            V((3, R, I), F32),
            V((I, R), F32),
            V((R, F), F32),
            V((R, F), F32),
            V((F, R), F32),
            V((1, R), F32),
            V((1, R), F32),
            V((BR, heads), F32),
            V((T, T), jnp.int32),
            V((1, T), jnp.int32),
        ]
        + [V(s.shape, s.dtype) for s in shapes]
        + [
            pltpu.SemaphoreType.DMA((13,)),
            pltpu.SemaphoreType.DMA((12,)),
            pltpu.SemaphoreType.DMA((12 * (Z - 1 + Z * (Y - 1)),)),
        ],
        compiler_params=pltpu.CompilerParams(
            collective_id=0, has_side_effects=True, vmem_limit_bytes=60 << 20
        ),
        name="gather_attend",
    )(
        tokens,
        w_query,
        w_key,
        w_value,
        w_out,
        w_gate,
        w_up,
        w_down,
        norm_attn.reshape(1, R),
        norm_ffn.reshape(1, R),
        bias_table,
        buckets,
        padding,
    )
    wa = wa.reshape(D, 3 * I)
    query_full, key_full, value_full = wa[:, :I], wa[:, I : 2 * I], wa[:, 2 * I :]
    out_t, gate_full, up_full, down_t = [w.reshape(D, -1) for w in (wo, wg, wu, wd)]
    gain_attn = misc[:, 0, :R].reshape(D).astype(BF).astype(F32)
    gain_ffn = misc[:, 1, :R].reshape(D).astype(BF).astype(F32)
    inputs = tokens.astype(F32)
    head_mix = jnp.transpose(o, (1, 0, 2)).reshape(T, I).astype(BF)
    middle = inputs + lax.psum(dot(head_mix, out_t, NT), "tensor")
    normed_ffn_low = rms_scale(middle, gain_ffn).astype(BF)
    gate_proj = dot(normed_ffn_low, gate_full, NN)
    up_proj = dot(normed_ffn_low, up_full, NN)
    hidden = gated_unit(gate_proj, up_proj).astype(BF)
    ffn_out = lax.psum(dot(hidden, down_t, NT).astype(BF), "tensor").astype(F32)
    block_out = (middle + ffn_out).astype(BF)
    grad_top = cotangent.astype(F32)
    grad_down = dot(cotangent, hidden, TN)
    grad_hidden = dot(cotangent, down_t, NN)
    _, unit_pull = jax.vjp(gated_unit, gate_proj, up_proj)
    grad_gate_act, grad_up_act = unit_pull(grad_hidden)
    grad_gate_low = grad_gate_act.astype(BF)
    grad_up_low = grad_up_act.astype(BF)
    grad_gate = dot(normed_ffn_low, grad_gate_low, TN)
    grad_up = dot(normed_ffn_low, grad_up_low, TN)
    partial_ffn = dot(grad_gate_low, gate_full, NT) + dot(grad_up_low, up_full, NT)
    grad_normed_ffn = lax.psum(partial_ffn, "tensor")
    _, norm_pull = jax.vjp(rms_scale, middle, gain_ffn)
    grad_middle_norm, grad_norm_ffn = norm_pull(grad_normed_ffn)
    grad_middle = grad_top + grad_middle_norm
    grad_middle_low = grad_middle.astype(BF)
    grad_out = dot(grad_middle_low, head_mix, TN)
    grad_mix = dot(grad_middle_low, out_t, NN).astype(BF)
    do = jnp.transpose(grad_mix.reshape(T, heads, HD), (1, 0, 2))
    VM = pl.BlockSpec(memory_space=pltpu.VMEM)
    wide = 32 * 4 * heads
    dq, dk, dv, bg = pl.pallas_call(
        functools.partial(back_kernel, heads),
        out_shape=[
            S((heads, T, HD), BF),
            S((heads, T, HD), BF),
            S((heads, T, HD), BF),
            S((256, wide), F32),
        ],
        in_specs=[VM] * 7,
        out_specs=[VM] * 4,
        scratch_shapes=[V((heads, T, T), BF)],
        compiler_params=pltpu.CompilerParams(vmem_limit_bytes=60 << 20),
        name="attend_back",
    )(q, k, v, do, o, p, buckets)
    grad_bias = jnp.sum(bg.reshape(8, 32, 4, heads, 32), axis=(1, 4)).reshape(BUCKETS, heads)
    flat = lambda a: jnp.transpose(a, (1, 0, 2)).reshape(T, I)
    dq, dk, dv = flat(dq), flat(dk), flat(dv)
    partial_attn = dot(dq, query_full, NT) + dot(dk, key_full, NT) + dot(dv, value_full, NT)
    grad_normed_attn = lax.psum(partial_attn.astype(BF), "tensor").astype(F32)
    _, first_pull = jax.vjp(rms_scale, inputs, gain_attn)
    grad_inputs_norm, grad_norm_attn = first_pull(grad_normed_attn)
    input_grad = grad_middle + grad_inputs_norm
    packed = jnp.concatenate(
        [dot(normed_low, a, TN).astype(BF) for a in (dq, dk, dv)]
        + [a.astype(BF) for a in (grad_out, grad_gate, grad_up, grad_down)],
        axis=1,
    )
    summed = lax.psum_scatter(packed, "dp", scatter_dimension=0, tiled=True).astype(F32)
    cuts = [0, I, 2 * I, 3 * I, 4 * I, 4 * I + F, 4 * I + 2 * F, 4 * I + 3 * F]
    g_q, g_k, g_v, g_o, g_g, g_u, g_d = [summed[:, a:b] for a, b in zip(cuts, cuts[1:])]
    scatter = lambda a: lax.psum_scatter(
        a.astype(BF), "dp", scatter_dimension=0, tiled=True
    ).astype(F32)
    return (
        block_out,
        input_grad,
        g_q,
        g_k,
        g_v,
        g_o.T,
        g_g,
        g_u,
        g_d.T,
        scatter(grad_norm_attn),
        scatter(grad_norm_ffn),
        scatter(grad_bias),
    )


def solution(mesh):
    shards, halves = mesh.shape["dp"], mesh.shape["tensor"]
    X = halves // 2
    Y = X if shards % X == 0 else 1
    sizes = (shards // Y, Y, X)
    in_specs = (
        P("dp", None),
        P("dp", None),
        P("dp", "tensor"),
        P("dp", "tensor"),
        P("dp", "tensor"),
        P("tensor", "dp"),
        P("dp", "tensor"),
        P("dp", "tensor"),
        P("tensor", "dp"),
        P("dp"),
        P("dp"),
        P("dp", "tensor"),
        P(),
        P("dp", None),
    )
    out_specs = (
        P("dp", None),
        P("dp", None),
        P("dp", "tensor"),
        P("dp", "tensor"),
        P("dp", "tensor"),
        P("tensor", "dp"),
        P("dp", "tensor"),
        P("dp", "tensor"),
        P("tensor", "dp"),
        P("dp"),
        P("dp"),
        P("dp", "tensor"),
    )
    return jax.shard_map(
        functools.partial(per_device, sizes),
        mesh=mesh,
        in_specs=in_specs,
        out_specs=out_specs,
        check_vma=False,
    )
```

```python
import functools
import types

import jax
import jax.numpy as jnp
from jax import lax
from jax.experimental import pallas as pl
from jax.experimental.pallas import tpu as pltpu
from jax.sharding import PartitionSpec as P

MESH = pl.DeviceIdType.MESH
BF = jnp.bfloat16
F32 = jnp.float32
NN = (((1,), (0,)), ((), ()))
NT = (((1,), (1,)), ((), ()))
TN = (((0,), (0,)), ((), ()))
epsilon = 1e-06
masked_score = -1000000000.0
LANES = 128
BUCKETS = 32
LOW = 4
GROUP = 32
BLOCK = 256
SUB = 128
gelu_scale = 0.7978845608028654
gelu_cube = 0.044715


def dot(former, latter, dims, **more):
    return lax.dot_general(former, latter, dims, preferred_element_type=F32, **more)


def rows_of(index, size):
    return pl.ds(pl.multiple_of(index * size, size), size)


def lookup(table, ids):
    tiles = ids.shape[1] // LANES
    return jnp.concatenate(
        [
            jnp.take_along_axis(table, ids[:, c * LANES : (c + 1) * LANES], axis=1)
            for c in range(tiles)
        ],
        axis=1,
    )


def inverse_rms(values):
    return lax.rsqrt(jnp.mean(values * values, axis=1, keepdims=True) + epsilon)


def norm_back(grad_normed, values, gain):
    r = inverse_rms(values)
    u = grad_normed * gain
    return r * u - values * (r * r * r) * jnp.mean(u * values, axis=1, keepdims=True)


class Comm:
    def __init__(self, sizes, sems):
        self.Z, self.Y, self.X = sizes
        self.sems = sems
        self.used = 0
        self.d, self.t = lax.axis_index("dp"), lax.axis_index("tensor")
        self.z, self.y = self.d // self.Y, self.d % self.Y
        self.x, self.c = self.t // 2, self.t % 2
        self.pending = []

    def z_peer(self, k):
        return ((self.z + k) % self.Z) * self.Y + self.y, self.t

    def y_peer(self, j):
        return self.z * self.Y + (self.y + j) % self.Y, self.t

    def x_to(self, j, other=0):
        core = self.c if other == 0 else 1 - self.c
        return ((self.x + j) % self.X) * 2 + core

    def x_from(self, j, other=0):
        core = self.c if other == 0 else 1 - self.c
        return ((self.x - j) % self.X) * 2 + core

    def origin(self, kz, j=0):
        return ((self.z - kz) % self.Z) * self.Y + (self.y - j) % self.Y

    def pair(self):
        self.used += 2
        return self.sems.at[self.used - 2], self.sems.at[self.used - 1]

    def barrier(self):
        peers = [self.z_peer(k) for k in range(1, self.Z)]
        peers += [self.y_peer(j) for j in range(1, self.Y)]
        peers += [(self.d, self.x_to(j)) for j in range(1, self.X)]
        peers += [(self.d, self.x_to(j, 1)) for j in range(self.X)]
        semaphore = pltpu.get_barrier_semaphore()
        for peer in peers:
            pl.semaphore_signal(semaphore, inc=1, device_id=peer, device_id_type=MESH)
        pl.semaphore_wait(semaphore, len(peers))

    def copy(self, src, dst, peer, pair):
        return pltpu.make_async_remote_copy(
            src_ref=src,
            dst_ref=dst,
            send_sem=pair[0],
            recv_sem=pair[1],
            device_id=peer,
            device_id_type=MESH,
        )

    def send(self, src, dst, peer, pair):
        made = self.copy(src, dst, peer, pair)
        made.start()
        self.pending.append(made)

    def arrived(self, ref, peer, pair):
        self.copy(ref, ref, peer, pair).wait_recv()

    def drain(self):
        for made in self.pending:
            made.wait_send()
        self.pending = []


class Gather:
    def __init__(self, comm, full):
        self.comm, self.full = comm, full
        Z, Y = comm.Z, comm.Y
        self.zp = {k: comm.pair() for k in range(1, Z)}
        self.yp = {(k, j): comm.pair() for k in range(Z) for j in range(1, Y)}

    def send_y(self, k):
        m = self.comm
        block = self.full.at[m.origin(k)]
        for j in range(1, m.Y):
            m.send(block, block, m.y_peer(j), self.yp[k, j])

    def start(self):
        m = self.comm
        own = self.full.at[m.d]
        for k in range(m.Z - 1, 0, -1):
            m.send(own, own, m.z_peer(k), self.zp[k])
        self.send_y(0)

    def forward(self):
        m = self.comm
        for k in range(1, m.Z):
            m.arrived(self.full.at[m.origin(k)], m.z_peer(k), self.zp[k])
            self.send_y(k)

    def finish(self):
        m = self.comm
        for k in range(m.Z):
            for j in range(1, m.Y):
                m.arrived(self.full.at[m.origin(k, j)], m.y_peer(j), self.yp[k, j])


class Share:
    def __init__(self, comm, part):
        self.comm, self.part = comm, part
        self.xp = {j: comm.pair() for j in range(1, comm.X)}
        self.cp = {j: comm.pair() for j in range(comm.X)}

    def send_core(self, j):
        m = self.comm
        ref = self.part(m.x_from(j))
        m.send(ref, ref, (m.d, m.x_to(0, 1)), self.cp[j])

    def start(self):
        m = self.comm
        ref = self.part(m.t)
        for j in range(1, m.X):
            m.send(ref, ref, (m.d, m.x_to(j)), self.xp[j])
        self.send_core(0)

    def forward(self):
        m = self.comm
        for j in range(1, m.X):
            m.arrived(self.part(m.x_from(j)), (m.d, m.x_to(j)), self.xp[j])
            self.send_core(j)

    def finish(self):
        m = self.comm
        for j in range(m.X):
            m.arrived(self.part(m.x_from(j, 1)), (m.d, m.x_to(0, 1)), self.cp[j])


class Scatter:
    def __init__(self, comm, part, from_y, mine, from_z):
        self.comm, self.part, self.from_y, self.mine, self.from_z = comm, part, from_y, mine, from_z
        self.yp = {j: comm.pair() for j in range(1, comm.Y)}
        self.zp = {k: comm.pair() for k in range(1, comm.Z)}

    def start(self):
        m = self.comm
        for j in range(1, m.Y):
            src = self.part.at[:, (m.y + j) % m.Y]
            m.send(src, self.from_y.at[j - 1], m.y_peer(j), self.yp[j])

    def middle(self):
        m = self.comm
        for j in range(1, m.Y):
            m.arrived(self.from_y.at[j - 1], m.y_peer(j), self.yp[j])
        total = self.part[:, m.y].astype(F32)
        for j in range(1, m.Y):
            total = total + self.from_y[j - 1].astype(F32)
        self.mine[...] = total.astype(self.mine.dtype)
        for k in range(1, m.Z):
            m.send(self.mine.at[(m.z + k) % m.Z], self.from_z.at[k - 1], m.z_peer(k), self.zp[k])

    def finish(self):
        m = self.comm
        total = self.mine[m.z].astype(F32)
        for k in range(1, m.Z):
            m.arrived(self.from_z.at[k - 1], m.z_peer(k), self.zp[k])
            total = total + self.from_z[k - 1].astype(F32)
        return total


class Halves:
    def __init__(self, comm, block, away, kept, near, far):
        self.comm, self.block = comm, block
        self.away, self.kept, self.near, self.far = away, kept, near, far
        self.cp = comm.pair()
        self.xp = {j: comm.pair() for j in range(1, comm.X)}

    def start(self, values):
        m, b = self.comm, self.block
        half = BLOCK // 2
        self.away[b] = values[:half].astype(BF)
        self.kept[b] = values[half:]
        m.send(self.away.at[b], self.near.at[b], (m.d, m.x_to(0, 1)), self.cp)

    def middle(self):
        m, b = self.comm, self.block
        m.arrived(self.near.at[b], (m.d, m.x_to(0, 1)), self.cp)
        self.far[m.x, b] = (self.kept[b] + self.near[b].astype(F32)).astype(BF)
        for j in range(1, m.X):
            ref = self.far.at[m.x, b]
            m.send(ref, ref, (m.d, m.x_to(j)), self.xp[j])

    def finish(self):
        m, b = self.comm, self.block
        for j in range(1, m.X):
            m.arrived(self.far.at[(m.x - j) % m.X, b], (m.d, m.x_to(j)), self.xp[j])
        total = self.far[0, b].astype(F32)
        for j in range(1, m.X):
            total = total + self.far[j, b].astype(F32)
        return total


def layer_kernel(sizes, heads, names, *refs):
    r = types.SimpleNamespace(**dict(zip(names, refs)))
    T, D = r.x.shape
    dp, R, I = r.wq_all.shape[1:]
    F = r.wg.shape[2]
    NT_ = r.wq_all.shape[0]
    BR = BUCKETS // dp
    HD = I // heads
    NB = T // BLOCK
    half = BLOCK // 2
    sem_at = iter(range(1000))

    def local(src, dst):
        return pltpu.make_async_copy(src, dst, r.local_sems.at[next(sem_at)])

    early = [
        local(r.wq_in, r.s_attn.at[0]),
        local(r.wk_in, r.s_attn.at[1]),
        local(r.wv_in, r.s_attn.at[2]),
        local(r.ga_in, r.s_ga),
        local(r.gf_in, r.s_gf),
        local(r.bt_in, r.s_bt),
    ]
    load_o = local(r.wo_in, r.s_attn.at[3])
    load_f = [local(ref, r.s_ffn.at[n]) for n, ref in enumerate((r.wg_in, r.wu_in, r.wd_in))]
    load_x = local(r.x_in, r.x)
    load_b = local(r.bucket_in, r.buckets)
    load_p = local(r.pad_in, r.pad)
    load_g = local(r.g_in, r.g)
    for load in early + [load_o] + load_f + [load_x, load_b, load_p, load_g]:
        load.start()
    comm = Comm(sizes, r.sems)
    comm.barrier()
    d, t, c = comm.d, comm.t, comm.c
    attn_full = [ref.at[t] for ref in (r.wq_all, r.wk_all, r.wv_all)]
    g_qkv = [Gather(comm, f) for f in attn_full]
    g_misc = Gather(comm, r.misc)
    g_o = Gather(comm, r.wo_all.at[t])
    g_ffn = [Gather(comm, f) for f in (r.wg, r.wu, r.wd)]
    s_w = [
        Share(comm, lambda n, ref=ref: ref.at[n]) for ref in (r.wo_all, r.wq_all, r.wk_all, r.wv_all)
    ]
    s_mix = [Share(comm, lambda n, b=b: r.o_all.at[n, rows_of(b, BLOCK)]) for b in range(NB)]
    s_dq = [Share(comm, lambda n, b=b: r.dq_all.at[n, rows_of(b, BLOCK)]) for b in range(NB)]
    s_dk = Share(comm, lambda n: r.dk_all.at[n])
    s_dv = Share(comm, lambda n: r.dv_all.at[n])
    h_mid = [Halves(comm, b, r.m_away, r.m_kept, r.m_near, r.m_far) for b in range(NB)]
    h_out = [Halves(comm, b, r.f_away, r.f_kept, r.f_near, r.f_far) for b in range(NB)]
    p_dmb = [comm.pair() for _ in range(NB)]
    p_bo = [comm.pair() for _ in range(NB)]
    p_ig = [comm.pair() for _ in range(NB)]
    p_norm = {n: comm.pair() for n in range(1, NT_)}
    sc = {
        n: Scatter(comm, *[getattr(r, f"{kind}_{n}") for kind in ("part", "fy", "mine", "fz")])
        for n in "qkvogudm"
    }

    for load in early:
        load.wait()
    for n, ref in enumerate((r.wq_all, r.wk_all, r.wv_all)):
        ref[t, d] = r.s_attn[n].astype(BF)
    r.misc[d] = jnp.zeros(r.misc.shape[1:], F32)
    r.misc[d, 0:1, 0:R] = r.s_ga[...]
    r.misc[d, 1:2, 0:R] = r.s_gf[...]
    r.misc[d, 2 : 2 + heads, 0:BR] = r.s_bt[...]
    g_misc.start()
    for g in g_qkv:
        g.start()
    load_o.wait()
    r.wo_all[t, d] = r.s_attn[3].astype(BF)
    g_o.start()
    for n, (load, ref, g) in enumerate(zip(load_f, (r.wg, r.wu, r.wd), g_ffn)):
        load.wait()
        ref[d] = r.s_ffn[n].astype(BF)
        g.start()
    load_x.wait()
    load_b.wait()
    load_p.wait()
    load_g.wait()
    g_misc.forward()
    for g in g_qkv:
        g.forward()
    g_misc.finish()
    gains = jnp.concatenate([r.misc[n, :, 0:R] for n in range(dp)], axis=1).astype(BF).astype(F32)
    gain_attn, gain_ffn = gains[0:1], gains[1:2]
    lane = lax.broadcasted_iota(jnp.int32, (8, LANES), 1)
    table = jnp.zeros((8, LANES), F32)
    for n in range(dp):
        moved = r.misc[n] if n == 0 else pltpu.roll(r.misc[n], n * BR, 1)
        table = jnp.where(lane // BR == n, moved, table)
    table = table.astype(BF).astype(F32)[2 : 2 + heads]

    for g in g_qkv:
        g.finish()

    def project(b, carry):
        rows = rows_of(b, BLOCK)
        x = r.x[rows, :].astype(F32)
        n1 = (x * inverse_rms(x) * gain_attn).astype(BF)
        r.n1[rows, :] = n1
        for full, out in zip(attn_full, (r.q, r.k, r.v)):
            made = dot(n1, full[...].reshape(D, I), NN).astype(BF)
            for h in range(heads):
                out[h, rows, :] = made[:, h * HD : (h + 1) * HD]
        return carry

    lax.fori_loop(0, NB, project, 0)
    g_o.forward()
    g_ffn[0].forward()
    real = r.pad[...] > 0

    def attend(i, carry):
        rows = rows_of(i, SUB)
        ids = r.buckets[rows, :]
        mixed = []
        for h in range(heads):
            scores = dot(r.q[h, rows, :], r.k[h], NT)
            bias = lookup(jnp.broadcast_to(table[h : h + 1, :], (SUB, LANES)), ids)
            scores = jnp.where(real, scores + bias, masked_score)
            top = jnp.max(scores, axis=1, keepdims=True)
            e = jnp.exp(scores - top)
            p = (e * (1.0 / jnp.sum(e, axis=1, keepdims=True))).astype(BF)
            r.p[h, rows, :] = p
            mix = dot(p, r.v[h], NN)
            r.o[h, rows, :] = mix
            mixed.append(mix.astype(BF))
        r.o_all[t, rows, :] = jnp.concatenate(mixed, axis=1)
        return carry

    steps = BLOCK // SUB
    for b in range(NB):
        lax.fori_loop(b * steps, (b + 1) * steps, attend, 0)
        s_mix[b].start()
        if b > 0:
            s_mix[b - 1].forward()
        if b == 0:
            g_ffn[1].forward()
            g_o.finish()
            s_w[0].start()
        if b == 1:
            g_ffn[2].forward()
            s_w[0].forward()
        if b == 2:
            for s in s_w[1:]:
                s.start()
    s_w[0].finish()
    for n in range(NT_):
        r.wo_cat[:, n * I : (n + 1) * I] = r.wo_all[n].reshape(D, I)
    s_mix[NB - 1].forward()
    for g in g_ffn:
        g.finish()

    def feed(b):
        s_mix[b].finish()
        halves = [rows_of(2 * b + 1 - c, half), rows_of(2 * b + c, half)]

        def both(ref):
            return jnp.concatenate([ref[rows, :] for rows in halves], axis=0)

        def put(ref, values):
            ref[halves[0], :] = values[:half]
            ref[halves[1], :] = values[half:]

        mixed = jnp.concatenate(
            [
                jnp.concatenate([r.o_all[n, rows, :] for n in range(NT_)], axis=1)
                for rows in halves
            ],
            axis=0,
        )
        middle = both(r.x).astype(F32) + dot(mixed, r.wo_cat[...], NT)
        r.mid[b] = middle[half:]
        n2 = (middle * inverse_rms(middle) * gain_ffn).astype(BF)
        put(r.n2, n2)
        w_gate, w_up, w_down = [w[...].reshape(D, F) for w in (r.wg, r.wu, r.wd)]
        gate = dot(n2, w_gate, NN)
        up = dot(n2, w_up, NN)
        square = gate * gate
        th = jnp.tanh(gelu_scale * gate * (1.0 + gelu_cube * square))
        left = 0.5 * (1.0 + th)
        active = gate * left
        slope = left + 0.5 * gate * (1.0 - th * th) * (
            gelu_scale * (1.0 + 3.0 * gelu_cube * square)
        )
        hidden = (active * up).astype(BF)
        put(r.hidden, hidden)
        dhidden = dot(both(r.g), w_down, NN)
        dgate = (dhidden * up * slope).astype(BF)
        dup = (dhidden * active).astype(BF)
        put(r.dgate, dgate)
        put(r.dup, dup)
        h_mid[b].start(dot(dgate, w_gate, NT) + dot(dup, w_up, NT))
        h_out[b].start(dot(hidden, w_down, NT))

    def to_middle(b):
        rows = rows_of(2 * b + c, half)
        dn2 = h_mid[b].finish()
        dmiddle = r.g[rows, :].astype(F32) + norm_back(dn2, r.mid[b], gain_ffn)
        r.dmid[b] = dmiddle
        r.dmb[rows, :] = dmiddle.astype(BF)
        ref = r.dmb.at[rows]
        comm.send(ref, ref, (d, comm.x_to(0, 1)), p_dmb[b])

    def scatter_grad(name, values):
        part = getattr(r, "part_" + name)
        part[...] = values.astype(BF).reshape(part.shape)
        sc[name].start()

    for b in range(NB):
        feed(b)
        if b >= 1:
            h_mid[b - 1].middle()
        if b >= 2:
            to_middle(b - 2)
    scatter_grad("d", dot(r.g[...], r.hidden[...], TN))
    h_mid[NB - 1].middle()
    scatter_grad("g", dot(r.n2[...], r.dgate[...], TN))
    to_middle(NB - 2)
    scatter_grad("u", dot(r.n2[...], r.dup[...], TN))
    to_middle(NB - 1)
    for b in range(NB):
        h_out[b].middle()
    for s in s_w[1:]:
        s.forward()
    sc["d"].middle()
    for b in range(NB):
        comm.arrived(r.dmb.at[rows_of(2 * b + 1 - c, half)], (d, comm.x_to(0, 1)), p_dmb[b])

    w_out = r.wo_all[t].reshape(D, I)

    def mix_grad(b, carry):
        rows = rows_of(b, BLOCK)
        do = dot(r.dmb[rows, :], w_out, NN).astype(BF)
        for h in range(heads):
            r.do[h, rows, :] = do[:, h * HD : (h + 1) * HD]
        return carry

    lax.fori_loop(0, NB, mix_grad, 0)
    r.dv_all[t] = jnp.concatenate(
        [dot(r.p[h], r.do[h], TN).astype(BF) for h in range(heads)], axis=1
    )
    s_dv.start()
    scatter_grad("o", dot(r.dmb[...], r.o_all[t], TN))
    sc["g"].middle()
    scatter_grad("v", dot(r.n1[...], r.dv_all[t], TN))

    def back(i, carry):
        rows = rows_of(i, SUB)
        made = []
        for h in range(heads):
            do = r.do[h, rows, :]
            delta = jnp.sum(do.astype(F32) * r.o[h, rows, :], axis=1, keepdims=True)
            dprob = dot(do, r.v[h], NT)
            ds = (r.p[h, rows, :].astype(F32) * (dprob - delta)).astype(BF)
            r.ds[h, rows, :] = ds
            made.append(dot(ds, r.k[h], NN).astype(BF))
        r.dq_all[t, rows, :] = jnp.concatenate(made, axis=1)
        return carry

    def block_out(b):
        total = h_out[b].finish() + r.mid[b]
        r.s_bo[b] = total.astype(BF)
        ref = r.block_out.at[rows_of(2 * b + c, half)]
        comm.send(r.s_bo.at[b], ref, (d, comm.x_to(0, 1)), p_bo[b])
        return local(r.s_bo.at[b], ref)

    stores = []
    for b in range(NB):
        lax.fori_loop(b * steps, (b + 1) * steps, back, 0)
        s_dq[b].start()
        if b == 0:
            sc["u"].middle()
            s_dv.forward()
        if b == 1:
            sc["o"].middle()
        if b == 2:
            sc["v"].middle()
        if b > 0:
            s_dq[b - 1].forward()
        stores.append(block_out(b))
        stores[-1].start()
    r.dk_all[t] = jnp.concatenate(
        [dot(r.ds[h], r.q[h], TN).astype(BF) for h in range(heads)], axis=1
    )
    s_dk.start()
    scatter_grad("k", dot(r.n1[...], r.dk_all[t], TN))
    scatter_grad("q", dot(r.n1[...], r.dq_all[t], TN))
    s_dq[NB - 1].forward()

    r.bias_sum[...] = jnp.zeros(r.bias_sum.shape, F32)

    def bias_rows(i, carry):
        rows = rows_of(i, GROUP)
        ids = r.buckets[rows, :]
        high = (ids // LOW).astype(BF)
        low = (ids % LOW).astype(BF)
        one, zero = jnp.ones_like(high), jnp.zeros_like(high)
        former = jnp.concatenate(
            [jnp.where(high == BF(n), one, zero) for n in range(BUCKETS // LOW)], axis=0
        )
        latter = []
        for n in range(LOW):
            match = low == BF(n)
            latter += [jnp.where(match, r.ds[h, rows, :], zero) for h in range(heads)]
        r.bias_sum[...] += dot(former, jnp.concatenate(latter, axis=0), NT)
        return carry

    groups = T // GROUP
    lax.fori_loop(0, groups // 2, bias_rows, 0)
    s_dk.forward()
    lax.fori_loop(groups // 2, groups, bias_rows, 0)
    exact = dict(precision=lax.Precision.HIGHEST)
    tall, wide = r.bias_sum.shape
    row = lax.broadcasted_iota(jnp.int32, (tall, wide), 0)
    column = lax.broadcasted_iota(jnp.int32, (tall, wide), 1)
    sums = jnp.where(row % GROUP == column % GROUP, r.bias_sum[...], 0.0)
    sums = jnp.sum(sums.reshape(BUCKETS // LOW, GROUP, wide), axis=1)
    bucket = lax.broadcasted_iota(jnp.int32, (LANES, BUCKETS // LOW), 0)
    high = lax.broadcasted_iota(jnp.int32, (LANES, BUCKETS // LOW), 1)
    spread = jnp.where(bucket // LOW == high, 1.0, 0.0)
    spread = dot(spread, sums, NN, **exact)
    bucket = lax.broadcasted_iota(jnp.int32, (LANES, wide), 0)
    column = lax.broadcasted_iota(jnp.int32, (LANES, wide), 1)
    spread = jnp.where(bucket % LOW == column // (heads * GROUP), spread, 0.0)
    head = lax.broadcasted_iota(jnp.int32, (8, wide), 0)
    column = lax.broadcasted_iota(jnp.int32, (8, wide), 1)
    of_head = jnp.where(column // GROUP % heads == head, 1.0, 0.0)
    by_head = dot(of_head, spread, NT, **exact)
    for n in range(dp):
        moved = by_head if n == 0 else pltpu.roll(by_head, LANES - n * BR, 1)
        r.part_m[n // comm.Y, n % comm.Y] = moved
    sc["m"].start()
    sc["k"].middle()
    sc["q"].middle()

    for s in s_w[1:]:
        s.finish()
    s_dv.finish()
    for s in s_dq:
        s.finish()
    s_dk.finish()
    for b in range(NB):
        rows = rows_of(2 * b + c, half)
        dn1 = jnp.zeros((half, D), F32)
        for full, grads in zip((r.wq_all, r.wk_all, r.wv_all), (r.dq_all, r.dk_all, r.dv_all)):
            former = jnp.concatenate([grads[n, rows, :] for n in range(NT_)], axis=1)
            latter = jnp.concatenate([full[n].reshape(D, I) for n in range(NT_)], axis=1)
            dn1 = dn1 + dot(former, latter, NT)
        x = r.x[rows, :].astype(F32)
        r.s_ig[b] = r.dmid[b] + norm_back(dn1, x, gain_attn)
        ref = r.input_grad.at[rows]
        comm.send(r.s_ig.at[b], ref, (d, comm.x_to(0, 1)), p_ig[b])
        stores.append(local(r.s_ig.at[b], ref))
        stores[-1].start()
        if b == 0:
            sc["m"].middle()

    outs = {}
    for n, out in zip("dguovkq", (r.o_d, r.o_g, r.o_u, r.o_o, r.o_v, r.o_k, r.o_q)):
        value = sc[n].finish()
        ref = getattr(r, "s_" + n)
        ref[...] = value
        outs[n] = value
        stores.append(local(ref, out))
        stores[-1].start()

    def gain_grad(pairs, gain):
        total = jnp.zeros((8, R), F32)
        for weight, grad in pairs:
            product = weight.astype(F32) * grad
            total = total + dot(jnp.ones((8, product.shape[1]), F32), product, NT, **exact)
        return total[0:1] / gain.astype(BF).astype(F32)

    own = [ref[t, d] for ref in (r.wq_all, r.wk_all, r.wv_all)]
    r.norm[t] = jnp.zeros(r.norm.shape[1:], F32)
    r.norm[t, 0:1, 0:R] = gain_grad(list(zip(own, [outs[n] for n in "qkv"])), r.s_ga[...])
    r.norm[t, 1:2, 0:R] = gain_grad([(r.wg[d], outs["g"]), (r.wu[d], outs["u"])], r.s_gf[...])
    for n in range(1, NT_):
        ref = r.norm.at[t]
        comm.send(ref, ref, (d, (t + n) % NT_), p_norm[n])
    r.s_m[...] = sc["m"].finish()[0:heads, 0:BR]
    stores.append(local(r.s_m, r.o_m))
    stores[-1].start()
    for n in range(1, NT_):
        comm.arrived(r.norm.at[(t - n) % NT_], (d, (t + n) % NT_), p_norm[n])
    total = r.norm[0]
    for n in range(1, NT_):
        total = total + r.norm[n]
    r.s_na[...] = total[0:1, 0:R]
    r.s_nf[...] = total[1:2, 0:R]
    stores += [local(r.s_na, r.o_na), local(r.s_nf, r.o_nf)]
    for store in stores[-2:]:
        store.start()
    for b in range(NB):
        rows = rows_of(2 * b + 1 - c, half)
        comm.arrived(r.block_out.at[rows], (d, comm.x_to(0, 1)), p_bo[b])
        comm.arrived(r.input_grad.at[rows], (d, comm.x_to(0, 1)), p_ig[b])
    comm.drain()
    for store in stores:
        store.wait()


def per_device(
    sizes,
    tokens,
    cotangent,
    w_query,
    w_key,
    w_value,
    w_out,
    w_gate,
    w_up,
    w_down,
    norm_attn,
    norm_ffn,
    bias_table,
    buckets,
    padding,
):
    T, D = tokens.shape
    R, I = w_query.shape
    F = w_gate.shape[1]
    BR, heads = bias_table.shape
    HD = I // heads
    Z, Y, X = sizes
    dp, tensor = Z * Y, 2 * X
    NB, half = T // BLOCK, BLOCK // 2
    S, V = jax.ShapeDtypeStruct, pltpu.VMEM
    inputs = dict(
        x_in=tokens,
        g_in=cotangent,
        wq_in=w_query,
        wk_in=w_key,
        wv_in=w_value,
        wo_in=w_out.T,
        wg_in=w_gate,
        wu_in=w_up,
        wd_in=w_down.T,
        ga_in=norm_attn.reshape(1, R),
        gf_in=norm_ffn.reshape(1, R),
        bt_in=bias_table.T,
        bucket_in=buckets,
        pad_in=padding,
    )
    outputs = dict(
        block_out=S((T, D), BF),
        input_grad=S((T, D), F32),
        o_q=S((R, I), F32),
        o_k=S((R, I), F32),
        o_v=S((R, I), F32),
        o_o=S((R, I), F32),
        o_g=S((R, F), F32),
        o_u=S((R, F), F32),
        o_d=S((R, F), F32),
        o_na=S((1, R), F32),
        o_nf=S((1, R), F32),
        o_m=S((heads, BR), F32),
    )
    scratch = dict(
        s_attn=V((4, R, I), F32),
        s_ffn=V((3, R, F), F32),
        s_ga=V((1, R), F32),
        s_gf=V((1, R), F32),
        s_bt=V((heads, BR), F32),
        x=V((T, D), BF),
        g=V((T, D), BF),
        buckets=V((T, T), jnp.int32),
        pad=V((1, T), jnp.int32),
        misc=V((dp, 8, LANES), F32),
        wq_all=V((tensor, dp, R, I), BF),
        wk_all=V((tensor, dp, R, I), BF),
        wv_all=V((tensor, dp, R, I), BF),
        wo_all=V((tensor, dp, R, I), BF),
        wo_cat=V((D, tensor * I), BF),
        wg=V((dp, R, F), BF),
        wu=V((dp, R, F), BF),
        wd=V((dp, R, F), BF),
        n1=V((T, D), BF),
        q=V((heads, T, HD), BF),
        k=V((heads, T, HD), BF),
        v=V((heads, T, HD), BF),
        p=V((heads, T, T), BF),
        o=V((heads, T, HD), F32),
        o_all=V((tensor, T, I), BF),
        mid=V((NB, half, D), F32),
        n2=V((T, D), BF),
        hidden=V((T, F), BF),
        dgate=V((T, F), BF),
        dup=V((T, F), BF),
        m_away=V((NB, half, D), BF),
        m_kept=V((NB, half, D), F32),
        m_near=V((NB, half, D), BF),
        m_far=V((X, NB, half, D), BF),
        f_away=V((NB, half, D), BF),
        f_kept=V((NB, half, D), F32),
        f_near=V((NB, half, D), BF),
        f_far=V((X, NB, half, D), BF),
        dmid=V((NB, half, D), F32),
        dmb=V((T, D), BF),
        do=V((heads, T, HD), BF),
        ds=V((heads, T, T), BF),
        dq_all=V((tensor, T, I), BF),
        dk_all=V((tensor, T, I), BF),
        dv_all=V((tensor, T, I), BF),
        bias_sum=V((BUCKETS // LOW * GROUP, LOW * heads * GROUP), F32),
        s_bo=V((NB, half, D), BF),
        s_ig=V((NB, half, D), F32),
        norm=V((tensor, 8, LANES), F32),
        s_m=V((heads, BR), F32),
        s_na=V((1, R), F32),
        s_nf=V((1, R), F32),
    )
    widths = dict(q=I, k=I, v=I, o=I, g=F, u=F, d=F)
    for n, width in widths.items():
        scratch["part_" + n] = V((Z, Y, R, width), BF)
        scratch["fy_" + n] = V((Y - 1, Z, R, width), BF)
        scratch["mine_" + n] = V((Z, R, width), BF)
        scratch["fz_" + n] = V((Z - 1, R, width), BF)
        scratch["s_" + n] = V((R, width), F32)
    scratch["part_m"] = V((Z, Y, 8, LANES), F32)
    scratch["fy_m"] = V((Y - 1, Z, 8, LANES), F32)
    scratch["mine_m"] = V((Z, 8, LANES), F32)
    scratch["fz_m"] = V((Z - 1, 8, LANES), F32)
    gathers, shares = 8, 4 + 2 * NB + 2
    count = gathers * (Z - 1 + Z * (Y - 1)) + shares * (2 * X - 1) + 8 * (Y - 1 + Z - 1)
    count += 2 * NB * X + 3 * NB + tensor - 1
    scratch["local_sems"] = pltpu.SemaphoreType.DMA((14 + 2 * NB + 10,))
    scratch["sems"] = pltpu.SemaphoreType.DMA((2 * count,))
    names = [*inputs, *outputs, *scratch]
    made = pl.pallas_call(
        functools.partial(layer_kernel, sizes, heads, names),
        out_shape=list(outputs.values()),
        in_specs=[pl.BlockSpec(memory_space=pl.ANY)] * len(inputs),
        out_specs=[pl.BlockSpec(memory_space=pl.ANY)] * len(outputs),
        scratch_shapes=list(scratch.values()),
        compiler_params=pltpu.CompilerParams(
            collective_id=0, has_side_effects=True, vmem_limit_bytes=62 << 20
        ),
        name="layer",
    )(*inputs.values())
    out = dict(zip(outputs, made))
    return (
        out["block_out"],
        out["input_grad"],
        out["o_q"],
        out["o_k"],
        out["o_v"],
        out["o_o"].T,
        out["o_g"],
        out["o_u"],
        out["o_d"].T,
        out["o_na"].reshape(R),
        out["o_nf"].reshape(R),
        out["o_m"].T,
    )


def solution(mesh):
    shards, halves = mesh.shape["dp"], mesh.shape["tensor"]
    X = halves // 2
    Y = X if shards % X == 0 else 1
    sizes = (shards // Y, Y, X)
    in_specs = (
        P("dp", None),
        P("dp", None),
        P("dp", "tensor"),
        P("dp", "tensor"),
        P("dp", "tensor"),
        P("tensor", "dp"),
        P("dp", "tensor"),
        P("dp", "tensor"),
        P("tensor", "dp"),
        P("dp"),
        P("dp"),
        P("dp", "tensor"),
        P(),
        P("dp", None),
    )
    out_specs = (
        P("dp", None),
        P("dp", None),
        P("dp", "tensor"),
        P("dp", "tensor"),
        P("dp", "tensor"),
        P("tensor", "dp"),
        P("dp", "tensor"),
        P("dp", "tensor"),
        P("tensor", "dp"),
        P("dp"),
        P("dp"),
        P("dp", "tensor"),
    )
    return jax.shard_map(
        functools.partial(per_device, sizes),
        mesh=mesh,
        in_specs=in_specs,
        out_specs=out_specs,
        check_vma=False,
    )
```

```python
import functools
import types

import jax
import jax.numpy as jnp
from jax import lax
from jax.experimental import pallas as pl
from jax.experimental.pallas import tpu as pltpu
from jax.sharding import PartitionSpec as P

MESH = pl.DeviceIdType.MESH
BF = jnp.bfloat16
F32 = jnp.float32
NN = (((1,), (0,)), ((), ()))
NT = (((1,), (1,)), ((), ()))
TN = (((0,), (0,)), ((), ()))
epsilon = 1e-06
masked_score = -1000000000.0
LANES = 128
BUCKETS = 32
LOW = 4
GROUP = 32
BLOCK = 256
SUB = 128
GROUPS = 8
gelu_scale = 0.7978845608028654
gelu_cube = 0.044715


def dot(former, latter, dims, **more):
    return lax.dot_general(former, latter, dims, preferred_element_type=F32, **more)


def rows_of(index, size):
    return pl.ds(pl.multiple_of(index * size, size), size)


def lookup(table, ids):
    tiles = ids.shape[1] // LANES
    return jnp.concatenate(
        [
            jnp.take_along_axis(table, ids[:, c * LANES : (c + 1) * LANES], axis=1)
            for c in range(tiles)
        ],
        axis=1,
    )


def inverse_rms(values):
    return lax.rsqrt(jnp.mean(values * values, axis=1, keepdims=True) + epsilon)


def norm_back(grad_normed, values, gain):
    r = inverse_rms(values)
    u = grad_normed * gain
    return r * u - values * (r * r * r) * jnp.mean(u * values, axis=1, keepdims=True)


class Comm:
    def __init__(self, sizes, sems):
        self.Z, self.Y, self.X = sizes
        self.sems = sems
        self.used = 0
        self.d, self.t = lax.axis_index("dp"), lax.axis_index("tensor")
        self.z, self.y = self.d // self.Y, self.d % self.Y
        self.x, self.c = self.t // 2, self.t % 2
        self.place = self.y * self.Z + self.z + (self.y % 2) * (self.Z - 1 - 2 * self.z)
        self.pending = []

    def z_peer(self, k):
        return ((self.z + k) % self.Z) * self.Y + self.y, self.t

    def y_peer(self, j):
        return self.z * self.Y + (self.y + j) % self.Y, self.t

    def x_to(self, j, other=0):
        core = self.c if other == 0 else 1 - self.c
        return ((self.x + j) % self.X) * 2 + core

    def x_from(self, j, other=0):
        core = self.c if other == 0 else 1 - self.c
        return ((self.x - j) % self.X) * 2 + core

    def origin(self, kz, j=0):
        return ((self.z - kz) % self.Z) * self.Y + (self.y - j) % self.Y

    def ring(self, place):
        count = self.Z * self.Y
        place = (place + count) % count
        y, z = place // self.Z, place % self.Z
        return (z + (y % 2) * (self.Z - 1 - 2 * z)) * self.Y + y

    def pair(self):
        self.used += 2
        return self.sems.at[self.used - 2], self.sems.at[self.used - 1]

    def barrier(self):
        peers = [self.z_peer(k) for k in range(1, self.Z)]
        peers += [self.y_peer(j) for j in range(1, self.Y)]
        peers += [(self.d, self.x_to(j)) for j in range(1, self.X)]
        peers += [(self.d, self.x_to(j, 1)) for j in range(self.X)]
        peers += [(self.ring(self.place + n), self.t) for n in (1, -1)]
        semaphore = pltpu.get_barrier_semaphore()
        for peer in peers:
            pl.semaphore_signal(semaphore, inc=1, device_id=peer, device_id_type=MESH)
        pl.semaphore_wait(semaphore, len(peers))

    def copy(self, src, dst, peer, pair):
        return pltpu.make_async_remote_copy(
            src_ref=src,
            dst_ref=dst,
            send_sem=pair[0],
            recv_sem=pair[1],
            device_id=peer,
            device_id_type=MESH,
        )

    def send(self, src, dst, peer, pair):
        made = self.copy(src, dst, peer, pair)
        made.start()
        self.pending.append(made)

    def arrived(self, ref, peer, pair):
        self.copy(ref, ref, peer, pair).wait_recv()

    def drain(self):
        for made in self.pending:
            made.wait_send()
        self.pending = []


class Gather:
    def __init__(self, comm, full):
        self.comm, self.full = comm, full
        Z, Y = comm.Z, comm.Y
        self.zp = {k: comm.pair() for k in range(1, Z)}
        self.yp = {(k, j): comm.pair() for k in range(Z) for j in range(1, Y)}

    def send_y(self, k):
        m = self.comm
        block = self.full.at[m.origin(k)]
        for j in range(1, m.Y):
            m.send(block, block, m.y_peer(j), self.yp[k, j])

    def start(self):
        m = self.comm
        own = self.full.at[m.d]
        for k in range(m.Z - 1, 0, -1):
            m.send(own, own, m.z_peer(k), self.zp[k])
        self.send_y(0)

    def forward(self):
        m = self.comm
        for k in range(1, m.Z):
            m.arrived(self.full.at[m.origin(k)], m.z_peer(k), self.zp[k])
            self.send_y(k)

    def finish(self):
        m = self.comm
        for k in range(m.Z):
            for j in range(1, m.Y):
                m.arrived(self.full.at[m.origin(k, j)], m.y_peer(j), self.yp[k, j])


class Ring:
    def __init__(self, comm, full, turn):
        self.comm, self.full = comm, full
        count = comm.Z * comm.Y
        most, least = count // 2, count - 1 - count // 2
        self.reach = (most, least) if turn == 0 else (least, most)
        self.pairs = [[comm.pair() for _ in range(n)] for n in self.reach]

    def block(self, way, step):
        m = self.comm
        return self.full.at[m.ring(m.place - step if way == 0 else m.place + step)]

    def pass_on(self, way, step):
        m = self.comm
        if step < self.reach[way]:
            ref = self.block(way, step)
            peer = m.ring(m.place + 1 if way == 0 else m.place - 1), m.t
            m.send(ref, ref, peer, self.pairs[way][step])

    def start(self):
        for way in range(2):
            self.pass_on(way, 0)

    def step(self, step):
        m = self.comm
        for way in range(2):
            if step <= self.reach[way]:
                peer = m.ring(m.place + 1 if way == 0 else m.place - 1), m.t
                m.arrived(self.block(way, step), peer, self.pairs[way][step - 1])
                self.pass_on(way, step)


class Share:
    def __init__(self, comm, part):
        self.comm, self.part = comm, part
        self.xp = {j: comm.pair() for j in range(1, comm.X)}
        self.cp = {j: comm.pair() for j in range(comm.X)}

    def send_core(self, j):
        m = self.comm
        ref = self.part(m.x_from(j))
        m.send(ref, ref, (m.d, m.x_to(0, 1)), self.cp[j])

    def start(self):
        m = self.comm
        ref = self.part(m.t)
        for j in range(1, m.X):
            m.send(ref, ref, (m.d, m.x_to(j)), self.xp[j])
        self.send_core(0)

    def forward(self):
        m = self.comm
        for j in range(1, m.X):
            m.arrived(self.part(m.x_from(j)), (m.d, m.x_to(j)), self.xp[j])
            self.send_core(j)

    def finish(self):
        m = self.comm
        for j in range(m.X):
            m.arrived(self.part(m.x_from(j, 1)), (m.d, m.x_to(0, 1)), self.cp[j])


class Scatter:
    def __init__(self, comm, part, from_y, mine, from_z):
        self.comm, self.part, self.from_y, self.mine, self.from_z = comm, part, from_y, mine, from_z
        self.yp = {j: comm.pair() for j in range(1, comm.Y)}
        self.zp = {k: comm.pair() for k in range(1, comm.Z)}

    def start(self):
        m = self.comm
        for j in range(1, m.Y):
            src = self.part.at[:, (m.y + j) % m.Y]
            m.send(src, self.from_y.at[j - 1], m.y_peer(j), self.yp[j])

    def middle(self):
        m = self.comm
        for j in range(1, m.Y):
            m.arrived(self.from_y.at[j - 1], m.y_peer(j), self.yp[j])
        total = self.part[:, m.y].astype(F32)
        for j in range(1, m.Y):
            total = total + self.from_y[j - 1].astype(F32)
        self.mine[...] = total.astype(self.mine.dtype)
        for k in range(1, m.Z):
            m.send(self.mine.at[(m.z + k) % m.Z], self.from_z.at[k - 1], m.z_peer(k), self.zp[k])

    def finish(self):
        m = self.comm
        total = self.mine[m.z].astype(F32)
        for k in range(1, m.Z):
            m.arrived(self.from_z.at[k - 1], m.z_peer(k), self.zp[k])
            total = total + self.from_z[k - 1].astype(F32)
        return total


class Halves:
    def __init__(self, comm, block, away, kept, near, far):
        self.comm, self.block = comm, block
        self.away, self.kept, self.near, self.far = away, kept, near, far
        self.cp = comm.pair()
        self.xp = {j: comm.pair() for j in range(1, comm.X)}

    def start(self, values):
        m, b = self.comm, self.block
        half = BLOCK // 2
        self.away[b] = values[:half].astype(BF)
        self.kept[b] = values[half:]
        m.send(self.away.at[b], self.near.at[b], (m.d, m.x_to(0, 1)), self.cp)

    def middle(self):
        m, b = self.comm, self.block
        m.arrived(self.near.at[b], (m.d, m.x_to(0, 1)), self.cp)
        self.far[m.x, b] = (self.kept[b] + self.near[b].astype(F32)).astype(BF)
        for j in range(1, m.X):
            ref = self.far.at[m.x, b]
            m.send(ref, ref, (m.d, m.x_to(j)), self.xp[j])

    def finish(self):
        m, b = self.comm, self.block
        for j in range(1, m.X):
            m.arrived(self.far.at[(m.x - j) % m.X, b], (m.d, m.x_to(j)), self.xp[j])
        total = self.far[0, b].astype(F32)
        for j in range(1, m.X):
            total = total + self.far[j, b].astype(F32)
        return total


def layer_kernel(sizes, heads, names, *refs):
    r = types.SimpleNamespace(**dict(zip(names, refs)))
    T, D = r.x.shape
    dp, R, I3 = r.wa.shape
    I, F = r.wo_all.shape[3], r.wg.shape[2]
    NT_ = r.wo_all.shape[0]
    BR = BUCKETS // dp
    HD = I // heads
    NB = T // BLOCK
    half = BLOCK // 2
    sem_at = iter(range(1000))

    def local(src, dst):
        return pltpu.make_async_copy(src, dst, r.local_sems.at[next(sem_at)])

    early = [
        local(r.wq_in, r.s_attn.at[0]),
        local(r.wk_in, r.s_attn.at[1]),
        local(r.wv_in, r.s_attn.at[2]),
        local(r.ga_in, r.s_ga),
        local(r.gf_in, r.s_gf),
        local(r.bt_in, r.s_bt),
    ]
    load_o = local(r.wo_in, r.s_attn.at[3])
    load_f = [local(ref, r.s_ffn.at[n]) for n, ref in enumerate((r.wg_in, r.wu_in, r.wd_in))]
    load_b = local(r.bucket_in, r.buckets)
    load_p = local(r.pad_in, r.pad)
    load_x = local(r.x_in, r.x)
    load_g = local(r.g_in, r.g)
    for load in early + [load_o] + load_f + [load_b, load_p, load_x, load_g]:
        load.start()
    comm = Comm(sizes, r.sems)
    comm.barrier()
    d, t, c = comm.d, comm.t, comm.c
    partner = (d, comm.x_to(0, 1))
    g_misc, g_a, g_o = [Gather(comm, f) for f in (r.misc, r.wa, r.wo_all.at[t])]
    g_ffn = [Ring(comm, f, n % 2) for n, f in enumerate((r.wg, r.wu, r.wd))]
    s_wo = Share(comm, lambda n: r.wo_all.at[n])
    s_mix = [Share(comm, lambda n, b=b: r.o_all.at[n, rows_of(b, BLOCK)]) for b in range(NB)]
    h_mid = [Halves(comm, b, r.m_away, r.m_kept, r.m_near, r.m_far) for b in range(NB)]
    h_out = [Halves(comm, b, r.f_away, r.f_kept, r.f_near, r.f_far) for b in range(NB)]
    h_in = [Halves(comm, b, r.i_away, r.i_kept, r.i_near, r.i_far) for b in range(NB)]
    p_dmb = [comm.pair() for _ in range(NB)]
    p_bo = [comm.pair() for _ in range(NB)]
    p_ig = [comm.pair() for _ in range(NB)]
    p_norm = {n: comm.pair() for n in range(1, NT_)}
    sc = {
        n: Scatter(comm, *[getattr(r, f"{kind}_{n}") for kind in ("part", "fy", "mine", "fz")])
        for n in "aogudm"
    }

    for load in early:
        load.wait()
    for n in range(3):
        r.wa[d, :, n * I : (n + 1) * I] = r.s_attn[n].astype(BF)
    r.misc[d] = jnp.zeros(r.misc.shape[1:], F32)
    r.misc[d, 0:1, 0:R] = r.s_ga[...]
    r.misc[d, 1:2, 0:R] = r.s_gf[...]
    r.misc[d, 2 : 2 + heads, 0:BR] = r.s_bt[...]
    g_misc.start()
    g_a.start()
    load_o.wait()
    r.wo_all[t, d] = r.s_attn[3].astype(BF)
    g_o.start()
    for n, (load, ref, g) in enumerate(zip(load_f, (r.wg, r.wu, r.wd), g_ffn)):
        load.wait()
        ref[d] = r.s_ffn[n].astype(BF)
        g.start()
    load_b.wait()
    load_p.wait()

    def split_bucket(i, carry):
        rows = rows_of(i, SUB)
        ids = r.buckets[rows, :]
        r.high[rows, :] = (ids // LOW).astype(BF)
        r.low[rows, :] = (ids % LOW).astype(BF)
        return carry

    lax.fori_loop(0, T // SUB, split_bucket, 0)
    g_misc.forward()
    g_a.forward()
    g_misc.finish()
    gains = jnp.concatenate([r.misc[n, :, 0:R] for n in range(dp)], axis=1).astype(BF).astype(F32)
    gain_attn, gain_ffn = gains[0:1], gains[1:2]
    lane = lax.broadcasted_iota(jnp.int32, (8, LANES), 1)
    table = jnp.zeros((8, LANES), F32)
    for n in range(dp):
        moved = r.misc[n] if n == 0 else pltpu.roll(r.misc[n], n * BR, 1)
        table = jnp.where(lane // BR == n, moved, table)
    table = table.astype(BF).astype(F32)[2 : 2 + heads]
    real = r.pad[...] > 0

    def fill_bias(i, carry):
        rows = rows_of(i, SUB)
        ids = r.buckets[rows, :]
        for h in range(heads):
            bias = lookup(jnp.broadcast_to(table[h : h + 1, :], (SUB, LANES)), ids)
            r.ds[h, rows, :] = jnp.where(real, bias, masked_score).astype(BF)
        return carry

    lax.fori_loop(0, T // SUB // 2, fill_bias, 0)
    g_o.forward()
    g_ffn[0].step(1)
    lax.fori_loop(T // SUB // 2, T // SUB, fill_bias, 0)
    g_ffn[1].step(1)
    load_x.wait()
    load_g.wait()

    g_a.finish()

    def project(b, carry):
        rows = rows_of(b, BLOCK)
        x = r.x[rows, :].astype(F32)
        n1 = (x * inverse_rms(x) * gain_attn).astype(BF)
        r.n1[rows, :] = n1
        made = dot(n1, r.wa[...].reshape(D, I3), NN).astype(BF)
        for n, out in enumerate((r.q, r.k, r.v)):
            for h in range(heads):
                out[h, rows, :] = made[:, n * I + h * HD : n * I + (h + 1) * HD]
        return carry

    lax.fori_loop(0, NB, project, 0)
    g_ffn[2].step(1)
    g_o.finish()
    s_wo.start()

    def mix(b):
        rows = slice(b * BLOCK, (b + 1) * BLOCK)
        return [dot(r.p[h, rows, :], r.v[h], NN) for h in range(heads)]

    def put_mix(b, mixed):
        rows = slice(b * BLOCK, (b + 1) * BLOCK)
        for h in range(heads):
            r.o[h, rows, :] = mixed[h]
        r.o_all[t, rows, :] = jnp.concatenate([m.astype(BF) for m in mixed], axis=1)
        s_mix[b].start()

    for b in range(NB):
        rows = slice(b * BLOCK, (b + 1) * BLOCK)
        mixed = mix(b - 1) if b > 0 else None
        weights = []
        for h in range(heads):
            scores = dot(r.q[h, rows, :], r.k[h], NT) + r.ds[h, rows, :].astype(F32)
            top = jnp.max(scores, axis=1, keepdims=True)
            e = jnp.exp(scores - top)
            weights.append((e * (1.0 / jnp.sum(e, axis=1, keepdims=True))).astype(BF))
        for h in range(heads):
            r.p[h, rows, :] = weights[h]
        if b > 0:
            put_mix(b - 1, mixed)
        if b == 0:
            g_ffn[0].step(2)
            g_ffn[1].step(2)
        if b == 1:
            g_ffn[2].step(2)
            s_wo.forward()
        if b == 2:
            g_ffn[0].step(3)
            s_mix[0].forward()
    put_mix(NB - 1, mix(NB - 1))
    g_ffn[1].step(3)
    s_mix[1].forward()
    g_ffn[2].step(3)
    s_mix[2].forward()
    s_wo.finish()
    for n in range(NT_):
        r.wo_cat[:, n * I : (n + 1) * I] = r.wo_all[n].reshape(D, I)
    g_ffn[0].step(4)
    s_mix[3].forward()
    g_ffn[1].step(4)
    g_ffn[2].step(4)
    for g in g_ffn:
        for step in range(5, dp // 2 + 1):
            g.step(step)

    def feed(b):
        s_mix[b].finish()
        halves = [rows_of(2 * b + 1 - c, half), rows_of(2 * b + c, half)]

        def both(ref):
            return jnp.concatenate([ref[rows, :] for rows in halves], axis=0)

        def put(ref, values):
            ref[halves[0], :] = values[:half]
            ref[halves[1], :] = values[half:]

        mixed = jnp.concatenate(
            [
                jnp.concatenate([r.o_all[n, rows, :] for n in range(NT_)], axis=1)
                for rows in halves
            ],
            axis=0,
        )
        middle = both(r.x).astype(F32) + dot(mixed, r.wo_cat[...], NT)
        r.mid[b] = middle[half:]
        n2 = (middle * inverse_rms(middle) * gain_ffn).astype(BF)
        put(r.n2, n2)
        w_gate, w_up, w_down = [w[...].reshape(D, F) for w in (r.wg, r.wu, r.wd)]
        gate = dot(n2, w_gate, NN)
        up = dot(n2, w_up, NN)
        square = gate * gate
        th = jnp.tanh(gelu_scale * gate * (1.0 + gelu_cube * square))
        left = 0.5 * (1.0 + th)
        active = gate * left
        slope = left + 0.5 * gate * (1.0 - th * th) * (
            gelu_scale * (1.0 + 3.0 * gelu_cube * square)
        )
        hidden = (active * up).astype(BF)
        put(r.hidden, hidden)
        dhidden = dot(both(r.g), w_down, NN)
        dgate = (dhidden * up * slope).astype(BF)
        dup = (dhidden * active).astype(BF)
        put(r.dgate, dgate)
        put(r.dup, dup)
        h_mid[b].start(dot(dgate, w_gate, NT) + dot(dup, w_up, NT))
        h_out[b].start(dot(hidden, w_down, NT))

    def to_middle(b):
        rows = rows_of(2 * b + c, half)
        dn2 = h_mid[b].finish()
        dmiddle = r.g[rows, :].astype(F32) + norm_back(dn2, r.mid[b], gain_ffn)
        r.dmid[b] = dmiddle
        r.dmb[rows, :] = dmiddle.astype(BF)
        ref = r.dmb.at[rows]
        comm.send(ref, ref, partner, p_dmb[b])

    def scatter_grad(name, values):
        part = getattr(r, "part_" + name)
        part[...] = values.astype(BF).reshape(part.shape)
        sc[name].start()

    w_out = r.wo_all[t].reshape(D, I)

    def back(b):
        comm.arrived(r.dmb.at[rows_of(2 * b + 1 - c, half)], partner, p_dmb[b])
        rows = slice(b * BLOCK, (b + 1) * BLOCK)
        do = dot(r.dmb[rows, :], w_out, NN).astype(BF)
        made = []
        for h in range(heads):
            do_h = do[:, h * HD : (h + 1) * HD]
            p = r.p[h, rows, :]
            delta = jnp.sum(do_h.astype(F32) * r.o[h, rows, :], axis=1, keepdims=True)
            ds = (p.astype(F32) * (dot(do_h, r.v[h], NT) - delta)).astype(BF)
            r.ds[h, rows, :] = ds
            made.append(dot(ds, r.k[h], NN).astype(BF))
            more_k, more_v = dot(ds, r.q[h, rows, :], TN), dot(p, do_h, TN)
            if b > 0:
                more_k, more_v = r.dk[h] + more_k, r.dv[h] + more_v
            r.dk[h], r.dv[h] = more_k, more_v
        r.da[rows, 0:I] = jnp.concatenate(made, axis=1)
        more = dot(r.dmb[rows, :], r.o_all[t, rows, :], TN)
        r.go[...] = more if b == 0 else r.go[...] + more

    for b in range(NB):
        feed(b)
        if b >= 1:
            h_mid[b - 1].middle()
    scatter_grad("d", dot(r.g[...], r.hidden[...], TN))
    h_mid[NB - 1].middle()
    scatter_grad("g", dot(r.n2[...], r.dgate[...], TN))
    to_middle(0)
    scatter_grad("u", dot(r.n2[...], r.dup[...], TN))
    for b in range(1, NB):
        to_middle(b)
        back(b - 1)
        if b == 2:
            sc["d"].middle()
    h_out[0].middle()
    back(NB - 1)
    r.da[:, I : 2 * I] = jnp.concatenate([r.dk[h].astype(BF) for h in range(heads)], axis=1)
    r.da[:, 2 * I : I3] = jnp.concatenate([r.dv[h].astype(BF) for h in range(heads)], axis=1)

    for b in range(NB):
        halves = [rows_of(2 * b + 1 - c, half), rows_of(2 * b + c, half)]
        former = jnp.concatenate([r.da[rows, :] for rows in halves], axis=0)
        h_in[b].start(dot(former, r.wa[...].reshape(D, I3), NT))
        if b >= 1:
            h_in[b - 1].middle()
    scatter_grad("a", dot(r.n1[...], r.da[...], TN))
    h_in[NB - 1].middle()
    scatter_grad("o", r.go[...])
    sc["g"].middle()
    for b in range(1, NB):
        h_out[b].middle()

    def bias_rows(i, carry):
        former, latter = [], []
        for g in range(GROUPS):
            rows = rows_of(i * GROUPS + g, GROUP)
            high, low = r.high[rows, :], r.low[rows, :]
            one, zero = jnp.ones_like(high), jnp.zeros_like(high)
            former.append(
                jnp.concatenate(
                    [jnp.where(high == BF(n), one, zero) for n in range(BUCKETS // LOW)], axis=0
                )
            )
            part = []
            for n in range(LOW):
                match = low == BF(n)
                part += [jnp.where(match, r.ds[h, rows, :], zero) for h in range(heads)]
            latter.append(jnp.concatenate(part, axis=0))
        return carry + dot(
            jnp.concatenate(former, axis=1), jnp.concatenate(latter, axis=1), NT
        )

    count = T // (GROUP * GROUPS)
    sums = lax.fori_loop(0, count // 2, bias_rows, jnp.zeros(r.bias_sum.shape, F32))
    r.bias_sum[...] = sums
    sc["a"].middle()
    sc["u"].middle()
    sums = r.bias_sum[...]
    sums = lax.fori_loop(count // 2, count, bias_rows, sums)
    exact = dict(precision=lax.Precision.HIGHEST)
    tall, wide = r.bias_sum.shape
    row = lax.broadcasted_iota(jnp.int32, (tall, wide), 0)
    column = lax.broadcasted_iota(jnp.int32, (tall, wide), 1)
    sums = jnp.where(row % GROUP == column % GROUP, sums, 0.0)
    sums = jnp.sum(sums.reshape(BUCKETS // LOW, GROUP, wide), axis=1)
    bucket = lax.broadcasted_iota(jnp.int32, (LANES, BUCKETS // LOW), 0)
    high = lax.broadcasted_iota(jnp.int32, (LANES, BUCKETS // LOW), 1)
    spread = jnp.where(bucket // LOW == high, 1.0, 0.0)
    spread = dot(spread, sums, NN, **exact)
    bucket = lax.broadcasted_iota(jnp.int32, (LANES, wide), 0)
    column = lax.broadcasted_iota(jnp.int32, (LANES, wide), 1)
    spread = jnp.where(bucket % LOW == column // (heads * GROUP), spread, 0.0)
    head = lax.broadcasted_iota(jnp.int32, (8, wide), 0)
    column = lax.broadcasted_iota(jnp.int32, (8, wide), 1)
    of_head = jnp.where(column // GROUP % heads == head, 1.0, 0.0)
    by_head = dot(of_head, spread, NT, **exact)
    for n in range(dp):
        moved = by_head if n == 0 else pltpu.roll(by_head, LANES - n * BR, 1)
        r.part_m[n // comm.Y, n % comm.Y] = moved
    sc["m"].start()
    sc["o"].middle()

    stores = []
    for b in range(NB):
        rows = rows_of(2 * b + c, half)
        x = r.x[rows, :].astype(F32)
        r.s_ig[b] = r.dmid[b] + norm_back(h_in[b].finish(), x, gain_attn)
        ref = r.input_grad.at[rows]
        comm.send(r.s_ig.at[b], ref, partner, p_ig[b])
        stores.append(local(r.s_ig.at[b], ref))
        stores[-1].start()
        if b == 0:
            sc["m"].middle()

    outs = {}

    def keep(name, value, out):
        ref = getattr(r, "s_" + name)
        ref[...] = value
        stores.append(local(ref, out))
        stores[-1].start()

    for n, out in zip("dgu", (r.o_d, r.o_g, r.o_u)):
        outs[n] = sc[n].finish()
        keep(n, outs[n], out)
    outs["a"] = sc["a"].finish()
    for n, name, out in zip(range(3), "qkv", (r.o_q, r.o_k, r.o_v)):
        keep(name, outs["a"][:, n * I : (n + 1) * I], out)

    def gain_grad(pairs, gain):
        total = jnp.zeros((8, R), F32)
        for weight, grad in pairs:
            product = weight.astype(F32) * grad
            total = total + dot(jnp.ones((8, product.shape[1]), F32), product, NT, **exact)
        return total[0:1] / gain.astype(BF).astype(F32)

    r.norm[t] = jnp.zeros(r.norm.shape[1:], F32)
    r.norm[t, 0:1, 0:R] = gain_grad([(r.wa[d], outs["a"])], r.s_ga[...])
    r.norm[t, 1:2, 0:R] = gain_grad([(r.wg[d], outs["g"]), (r.wu[d], outs["u"])], r.s_gf[...])
    for n in range(1, NT_):
        ref = r.norm.at[t]
        comm.send(ref, ref, (d, (t + n) % NT_), p_norm[n])
    keep("o", sc["o"].finish(), r.o_o)
    keep("m", sc["m"].finish()[0:heads, 0:BR], r.o_m)
    for b in range(NB):
        rows = rows_of(2 * b + c, half)
        total = h_out[b].finish() + r.mid[b]
        r.s_bo[b] = total.astype(BF)
        ref = r.block_out.at[rows]
        comm.send(r.s_bo.at[b], ref, partner, p_bo[b])
        stores.append(local(r.s_bo.at[b], ref))
        stores[-1].start()
    for n in range(1, NT_):
        comm.arrived(r.norm.at[(t - n) % NT_], (d, (t + n) % NT_), p_norm[n])
    total = r.norm[0]
    for n in range(1, NT_):
        total = total + r.norm[n]
    keep("na", total[0:1, 0:R], r.o_na)
    keep("nf", total[1:2, 0:R], r.o_nf)
    for b in range(NB):
        rows = rows_of(2 * b + 1 - c, half)
        comm.arrived(r.block_out.at[rows], partner, p_bo[b])
        comm.arrived(r.input_grad.at[rows], partner, p_ig[b])
    comm.drain()
    for store in stores:
        store.wait()


def hand_over(*refs):
    sems = refs[-1]
    count = (len(refs) - 1) // 3
    before, after, held = refs[:count], refs[count : 2 * count], refs[2 * count : 3 * count]
    loads = [
        pltpu.make_async_copy(a, b, sems.at[2 * n]) for n, (a, b) in enumerate(zip(before, held))
    ]
    stores = [
        pltpu.make_async_copy(a, b, sems.at[2 * n + 1]) for n, (a, b) in enumerate(zip(held, after))
    ]
    for load in loads:
        load.start()
    for load, store in zip(loads, stores):
        load.wait()
        store.start()
    for store in stores:
        store.wait()


def per_device(
    sizes,
    tokens,
    cotangent,
    w_query,
    w_key,
    w_value,
    w_out,
    w_gate,
    w_up,
    w_down,
    norm_attn,
    norm_ffn,
    bias_table,
    buckets,
    padding,
):
    T, D = tokens.shape
    R, I = w_query.shape
    F = w_gate.shape[1]
    BR, heads = bias_table.shape
    HD = I // heads
    Z, Y, X = sizes
    dp, tensor = Z * Y, 2 * X
    NB, half = T // BLOCK, BLOCK // 2
    S, V = jax.ShapeDtypeStruct, pltpu.VMEM
    inputs = dict(
        x_in=tokens,
        g_in=cotangent,
        wq_in=w_query,
        wk_in=w_key,
        wv_in=w_value,
        wo_in=w_out.T,
        wg_in=w_gate,
        wu_in=w_up,
        wd_in=w_down.T,
        ga_in=norm_attn.reshape(1, R),
        gf_in=norm_ffn.reshape(1, R),
        bt_in=bias_table.T,
        bucket_in=buckets,
        pad_in=padding,
    )
    outputs = dict(
        block_out=S((T, D), BF),
        input_grad=S((T, D), F32),
        o_q=S((R, I), F32),
        o_k=S((R, I), F32),
        o_v=S((R, I), F32),
        o_o=S((R, I), F32),
        o_g=S((R, F), F32),
        o_u=S((R, F), F32),
        o_d=S((R, F), F32),
        o_na=S((1, R), F32),
        o_nf=S((1, R), F32),
        o_m=S((heads, BR), F32),
    )
    scratch = dict(
        s_attn=V((4, R, I), F32),
        s_ffn=V((3, R, F), F32),
        s_ga=V((1, R), F32),
        s_gf=V((1, R), F32),
        s_bt=V((heads, BR), F32),
        x=V((T, D), BF),
        g=V((T, D), BF),
        buckets=V((T, T), jnp.int32),
        pad=V((1, T), jnp.int32),
        misc=V((dp, 8, LANES), F32),
        wa=V((dp, R, 3 * I), BF),
        high=V((T, T), BF),
        low=V((T, T), BF),
        wo_all=V((tensor, dp, R, I), BF),
        wo_cat=V((D, tensor * I), BF),
        wg=V((dp, R, F), BF),
        wu=V((dp, R, F), BF),
        wd=V((dp, R, F), BF),
        n1=V((T, D), BF),
        q=V((heads, T, HD), BF),
        k=V((heads, T, HD), BF),
        v=V((heads, T, HD), BF),
        p=V((heads, T, T), BF),
        o=V((heads, T, HD), F32),
        o_all=V((tensor, T, I), BF),
        mid=V((NB, half, D), F32),
        n2=V((T, D), BF),
        hidden=V((T, F), BF),
        dgate=V((T, F), BF),
        dup=V((T, F), BF),
        m_away=V((NB, half, D), BF),
        m_kept=V((NB, half, D), F32),
        m_near=V((NB, half, D), BF),
        m_far=V((X, NB, half, D), BF),
        f_away=V((NB, half, D), BF),
        f_kept=V((NB, half, D), F32),
        f_near=V((NB, half, D), BF),
        f_far=V((X, NB, half, D), BF),
        dmid=V((NB, half, D), F32),
        dmb=V((T, D), BF),
        i_away=V((NB, half, D), BF),
        i_kept=V((NB, half, D), F32),
        i_near=V((NB, half, D), BF),
        i_far=V((X, NB, half, D), BF),
        dk=V((heads, T, HD), F32),
        dv=V((heads, T, HD), F32),
        da=V((T, 3 * I), BF),
        go=V((D, I), F32),
        ds=V((heads, T, T), BF),
        bias_sum=V((BUCKETS // LOW * GROUP, LOW * heads * GROUP), F32),
        s_bo=V((NB, half, D), BF),
        s_ig=V((NB, half, D), F32),
        norm=V((tensor, 8, LANES), F32),
        s_m=V((heads, BR), F32),
        s_na=V((1, R), F32),
        s_nf=V((1, R), F32),
    )
    widths = dict(a=3 * I, o=I, g=F, u=F, d=F)
    for n, width in widths.items():
        scratch["part_" + n] = V((Z, Y, R, width), BF)
        scratch["fy_" + n] = V((Y - 1, Z, R, width), BF)
        scratch["mine_" + n] = V((Z, R, width), BF)
        scratch["fz_" + n] = V((Z - 1, R, width), BF)
    for n, width in dict(q=I, k=I, v=I, o=I, g=F, u=F, d=F).items():
        scratch["s_" + n] = V((R, width), F32)
    scratch["part_m"] = V((Z, Y, 8, LANES), F32)
    scratch["fy_m"] = V((Y - 1, Z, 8, LANES), F32)
    scratch["mine_m"] = V((Z, 8, LANES), F32)
    scratch["fz_m"] = V((Z - 1, 8, LANES), F32)
    count = 3 * (Z - 1 + Z * (Y - 1)) + 3 * (dp - 1) + (1 + NB) * (2 * X - 1)
    count += 3 * NB * X + 3 * NB + tensor - 1 + 6 * (Y + Z - 2)
    scratch["local_sems"] = pltpu.SemaphoreType.DMA((14 + 2 * NB + 10,))
    scratch["sems"] = pltpu.SemaphoreType.DMA((2 * count,))
    names = [*inputs, *outputs, *scratch]
    made = pl.pallas_call(
        functools.partial(layer_kernel, sizes, heads, names),
        out_shape=list(outputs.values()),
        in_specs=[pl.BlockSpec(memory_space=pl.ANY)] * len(inputs),
        out_specs=[pl.BlockSpec(memory_space=pl.ANY)] * len(outputs),
        scratch_shapes=list(scratch.values()),
        compiler_params=pltpu.CompilerParams(
            collective_id=0, has_side_effects=True, vmem_limit_bytes=62 << 20
        ),
        name="layer",
    )(*inputs.values())
    made = pl.pallas_call(
        hand_over,
        out_shape=list(outputs.values()),
        in_specs=[pl.BlockSpec(memory_space=pl.ANY)] * len(outputs),
        out_specs=[pl.BlockSpec(memory_space=pl.ANY)] * len(outputs),
        scratch_shapes=[V(o.shape, o.dtype) for o in outputs.values()]
        + [pltpu.SemaphoreType.DMA((2 * len(outputs),))],
        name="hand_over",
    )(*made)
    out = dict(zip(outputs, made))
    return (
        out["block_out"],
        out["input_grad"],
        out["o_q"],
        out["o_k"],
        out["o_v"],
        out["o_o"].T,
        out["o_g"],
        out["o_u"],
        out["o_d"].T,
        out["o_na"].reshape(R),
        out["o_nf"].reshape(R),
        out["o_m"].T,
    )


def solution(mesh):
    shards, halves = mesh.shape["dp"], mesh.shape["tensor"]
    X = halves // 2
    Y = X if shards % X == 0 else 1
    sizes = (shards // Y, Y, X)
    in_specs = (
        P("dp", None),
        P("dp", None),
        P("dp", "tensor"),
        P("dp", "tensor"),
        P("dp", "tensor"),
        P("tensor", "dp"),
        P("dp", "tensor"),
        P("dp", "tensor"),
        P("tensor", "dp"),
        P("dp"),
        P("dp"),
        P("dp", "tensor"),
        P(),
        P("dp", None),
    )
    out_specs = (
        P("dp", None),
        P("dp", None),
        P("dp", "tensor"),
        P("dp", "tensor"),
        P("dp", "tensor"),
        P("tensor", "dp"),
        P("dp", "tensor"),
        P("dp", "tensor"),
        P("tensor", "dp"),
        P("dp"),
        P("dp"),
        P("dp", "tensor"),
    )
    return jax.shard_map(
        functools.partial(per_device, sizes),
        mesh=mesh,
        in_specs=in_specs,
        out_specs=out_specs,
        check_vma=False,
    )
```

```python
import functools
import types

import jax
import jax.numpy as jnp
from jax import lax
from jax.experimental import pallas as pl
from jax.experimental.pallas import tpu as pltpu
from jax.sharding import PartitionSpec as P

MESH = pl.DeviceIdType.MESH
BF = jnp.bfloat16
F32 = jnp.float32
NN = (((1,), (0,)), ((), ()))
NT = (((1,), (1,)), ((), ()))
TN = (((0,), (0,)), ((), ()))
epsilon = 1e-06
masked_score = -1000000000.0
LANES = 128
BUCKETS = 32
LOW = 4
GROUP = 32
BLOCK = 256
SUB = 128
GROUPS = 8
gelu_scale = 0.7978845608028654
gelu_cube = 0.044715


def dot(former, latter, dims, **more):
    return lax.dot_general(former, latter, dims, preferred_element_type=F32, **more)


def rows_of(index, size):
    return pl.ds(pl.multiple_of(index * size, size), size)


def lookup(table, ids):
    tiles = ids.shape[1] // LANES
    return jnp.concatenate(
        [
            jnp.take_along_axis(table, ids[:, c * LANES : (c + 1) * LANES], axis=1)
            for c in range(tiles)
        ],
        axis=1,
    )


def inverse_rms(values):
    return lax.rsqrt(jnp.mean(values * values, axis=1, keepdims=True) + epsilon)


def norm_back(grad_normed, values, gain):
    r = inverse_rms(values)
    u = grad_normed * gain
    return r * u - values * (r * r * r) * jnp.mean(u * values, axis=1, keepdims=True)


class Comm:
    def __init__(self, sizes, sems):
        self.Z, self.Y, self.X = sizes
        self.sems = sems
        self.used = 0
        self.d, self.t = lax.axis_index("dp"), lax.axis_index("tensor")
        self.z, self.y = self.d // self.Y, self.d % self.Y
        self.x, self.c = self.t // 2, self.t % 2
        self.place = self.y * self.Z + self.z + (self.y % 2) * (self.Z - 1 - 2 * self.z)
        self.pending = []

    def z_peer(self, k):
        return ((self.z + k) % self.Z) * self.Y + self.y, self.t

    def y_peer(self, j):
        return self.z * self.Y + (self.y + j) % self.Y, self.t

    def x_to(self, j, other=0):
        core = self.c if other == 0 else 1 - self.c
        return ((self.x + j) % self.X) * 2 + core

    def x_from(self, j, other=0):
        core = self.c if other == 0 else 1 - self.c
        return ((self.x - j) % self.X) * 2 + core

    def origin(self, kz, j=0):
        return ((self.z - kz) % self.Z) * self.Y + (self.y - j) % self.Y

    def ring(self, place):
        count = self.Z * self.Y
        place = (place + count) % count
        y, z = place // self.Z, place % self.Z
        return (z + (y % 2) * (self.Z - 1 - 2 * z)) * self.Y + y

    def pair(self):
        self.used += 2
        return self.sems.at[self.used - 2], self.sems.at[self.used - 1]

    def barrier(self):
        peers = [self.z_peer(k) for k in range(1, self.Z)]
        peers += [self.y_peer(j) for j in range(1, self.Y)]
        peers += [(self.d, self.x_to(j)) for j in range(1, self.X)]
        peers += [(self.d, self.x_to(j, 1)) for j in range(self.X)]
        peers += [(self.ring(self.place + n), self.t) for n in (1, -1)]
        semaphore = pltpu.get_barrier_semaphore()
        for peer in peers:
            pl.semaphore_signal(semaphore, inc=1, device_id=peer, device_id_type=MESH)
        return lambda: pl.semaphore_wait(semaphore, len(peers))

    def copy(self, src, dst, peer, pair):
        return pltpu.make_async_remote_copy(
            src_ref=src,
            dst_ref=dst,
            send_sem=pair[0],
            recv_sem=pair[1],
            device_id=peer,
            device_id_type=MESH,
        )

    def send(self, src, dst, peer, pair):
        made = self.copy(src, dst, peer, pair)
        made.start()
        self.pending.append(made)

    def arrived(self, ref, peer, pair):
        self.copy(ref, ref, peer, pair).wait_recv()

    def drain(self):
        for made in self.pending:
            made.wait_send()
        self.pending = []


class Gather:
    def __init__(self, comm, full):
        self.comm, self.full = comm, full
        Z, Y = comm.Z, comm.Y
        self.zp = {k: comm.pair() for k in range(1, Z)}
        self.yp = {(k, j): comm.pair() for k in range(Z) for j in range(1, Y)}

    def send_y(self, k):
        m = self.comm
        block = self.full.at[m.origin(k)]
        for j in range(1, m.Y):
            m.send(block, block, m.y_peer(j), self.yp[k, j])

    def start(self):
        m = self.comm
        own = self.full.at[m.d]
        for k in range(m.Z - 1, 0, -1):
            m.send(own, own, m.z_peer(k), self.zp[k])
        self.send_y(0)

    def forward(self):
        m = self.comm
        for k in range(1, m.Z):
            m.arrived(self.full.at[m.origin(k)], m.z_peer(k), self.zp[k])
            self.send_y(k)

    def finish(self):
        m = self.comm
        for k in range(m.Z):
            for j in range(1, m.Y):
                m.arrived(self.full.at[m.origin(k, j)], m.y_peer(j), self.yp[k, j])


class Ring:
    def __init__(self, comm, full, turn):
        self.comm, self.full = comm, full
        count = comm.Z * comm.Y
        most, least = count // 2, count - 1 - count // 2
        self.reach = (most, least) if turn == 0 else (least, most)
        self.pairs = [[comm.pair() for _ in range(n)] for n in self.reach]

    def block(self, way, step):
        m = self.comm
        return self.full.at[m.ring(m.place - step if way == 0 else m.place + step)]

    def pass_on(self, way, step):
        m = self.comm
        if step < self.reach[way]:
            ref = self.block(way, step)
            peer = m.ring(m.place + 1 if way == 0 else m.place - 1), m.t
            m.send(ref, ref, peer, self.pairs[way][step])

    def start(self):
        for way in range(2):
            self.pass_on(way, 0)

    def step(self, step):
        m = self.comm
        for way in range(2):
            if step <= self.reach[way]:
                peer = m.ring(m.place + 1 if way == 0 else m.place - 1), m.t
                m.arrived(self.block(way, step), peer, self.pairs[way][step - 1])
                self.pass_on(way, step)


class Share:
    def __init__(self, comm, part):
        self.comm, self.part = comm, part
        self.xp = {j: comm.pair() for j in range(1, comm.X)}
        self.cp = {j: comm.pair() for j in range(comm.X)}

    def send_core(self, j):
        m = self.comm
        ref = self.part(m.x_from(j))
        m.send(ref, ref, (m.d, m.x_to(0, 1)), self.cp[j])

    def start(self):
        m = self.comm
        ref = self.part(m.t)
        for j in range(1, m.X):
            m.send(ref, ref, (m.d, m.x_to(j)), self.xp[j])
        self.send_core(0)

    def forward(self):
        m = self.comm
        for j in range(1, m.X):
            m.arrived(self.part(m.x_from(j)), (m.d, m.x_to(j)), self.xp[j])
            self.send_core(j)

    def finish(self):
        m = self.comm
        for j in range(m.X):
            m.arrived(self.part(m.x_from(j, 1)), (m.d, m.x_to(0, 1)), self.cp[j])


class Scatter:
    def __init__(self, comm, part, from_y, mine, from_z):
        self.comm, self.part, self.from_y, self.mine, self.from_z = comm, part, from_y, mine, from_z
        self.yp = {j: comm.pair() for j in range(1, comm.Y)}
        self.zp = {k: comm.pair() for k in range(1, comm.Z)}

    def start(self):
        m = self.comm
        for j in range(1, m.Y):
            src = self.part.at[:, (m.y + j) % m.Y]
            m.send(src, self.from_y.at[j - 1], m.y_peer(j), self.yp[j])

    def middle(self):
        m = self.comm
        for j in range(1, m.Y):
            m.arrived(self.from_y.at[j - 1], m.y_peer(j), self.yp[j])
        total = self.part[:, m.y].astype(F32)
        for j in range(1, m.Y):
            total = total + self.from_y[j - 1].astype(F32)
        self.mine[...] = total.astype(self.mine.dtype)
        for k in range(1, m.Z):
            m.send(self.mine.at[(m.z + k) % m.Z], self.from_z.at[k - 1], m.z_peer(k), self.zp[k])

    def finish(self):
        m = self.comm
        total = self.mine[m.z].astype(F32)
        for k in range(1, m.Z):
            m.arrived(self.from_z.at[k - 1], m.z_peer(k), self.zp[k])
            total = total + self.from_z[k - 1].astype(F32)
        return total


class Halves:
    def __init__(self, comm, block, away, kept, near, far):
        self.comm, self.block = comm, block
        self.away, self.kept, self.near, self.far = away, kept, near, far
        self.cp = comm.pair()
        self.xp = {j: comm.pair() for j in range(1, comm.X)}

    def start(self, values):
        m, b = self.comm, self.block
        half = BLOCK // 2
        self.away[b] = values[:half].astype(BF)
        self.kept[b] = values[half:]
        m.send(self.away.at[b], self.near.at[b], (m.d, m.x_to(0, 1)), self.cp)

    def middle(self):
        m, b = self.comm, self.block
        m.arrived(self.near.at[b], (m.d, m.x_to(0, 1)), self.cp)
        self.far[m.x, b] = (self.kept[b] + self.near[b].astype(F32)).astype(BF)
        for j in range(1, m.X):
            ref = self.far.at[m.x, b]
            m.send(ref, ref, (m.d, m.x_to(j)), self.xp[j])

    def finish(self):
        m, b = self.comm, self.block
        for j in range(1, m.X):
            m.arrived(self.far.at[(m.x - j) % m.X, b], (m.d, m.x_to(j)), self.xp[j])
        total = self.far[0, b].astype(F32)
        for j in range(1, m.X):
            total = total + self.far[j, b].astype(F32)
        return total


def layer_kernel(sizes, heads, names, *refs):
    r = types.SimpleNamespace(**dict(zip(names, refs)))
    T, D = r.x.shape
    dp, R, I3 = r.wa.shape
    I, F = r.wo_all.shape[3], r.wg.shape[2]
    NT_ = r.wo_all.shape[0]
    BR = BUCKETS // dp
    HD = I // heads
    NB = T // BLOCK
    half = BLOCK // 2
    sem_at = iter(range(1000))

    def local(src, dst):
        return pltpu.make_async_copy(src, dst, r.local_sems.at[next(sem_at)])

    early = [
        local(r.wq_in, r.s_attn.at[0]),
        local(r.wk_in, r.s_attn.at[1]),
        local(r.wv_in, r.s_attn.at[2]),
        local(r.ga_in, r.s_ga),
        local(r.gf_in, r.s_gf),
        local(r.bt_in, r.s_bt),
    ]
    load_o = local(r.wo_in, r.s_attn.at[3])
    load_f = [local(ref, r.s_ffn.at[n]) for n, ref in enumerate((r.wg_in, r.wu_in, r.wd_in))]
    load_b = local(r.bucket_in, r.buckets)
    load_p = local(r.pad_in, r.pad)
    load_x = local(r.x_in, r.x)
    load_g = local(r.g_in, r.g)
    for load in early + [load_o] + load_f + [load_b, load_p, load_x, load_g]:
        load.start()
    comm = Comm(sizes, r.sems)
    all_here = comm.barrier()
    d, t, c = comm.d, comm.t, comm.c
    partner = (d, comm.x_to(0, 1))
    g_misc, g_a, g_o = [Gather(comm, f) for f in (r.misc, r.wa, r.wo_all.at[t])]
    g_ffn = [Ring(comm, f, n % 2) for n, f in enumerate((r.wg, r.wu, r.wd))]
    s_wo = Share(comm, lambda n: r.wo_all.at[n])
    s_mix = [Share(comm, lambda n, b=b: r.o_all.at[n, rows_of(b, BLOCK)]) for b in range(NB)]
    h_mid = [Halves(comm, b, r.m_away, r.m_kept, r.m_near, r.m_far) for b in range(NB)]
    h_out = [Halves(comm, b, r.f_away, r.f_kept, r.f_near, r.f_far) for b in range(NB)]
    h_in = [Halves(comm, b, r.i_away, r.i_kept, r.i_near, r.i_far) for b in range(NB)]
    p_dmb = [comm.pair() for _ in range(NB)]
    p_bo = [comm.pair() for _ in range(NB)]
    p_ig = [comm.pair() for _ in range(NB)]
    p_norm = {n: comm.pair() for n in range(1, NT_)}
    sc = {
        n: Scatter(comm, *[getattr(r, f"{kind}_{n}") for kind in ("part", "fy", "mine", "fz")])
        for n in "aogudm"
    }

    for load in early:
        load.wait()
    for n in range(3):
        r.wa[d, :, n * I : (n + 1) * I] = r.s_attn[n].astype(BF)
    r.misc[d] = jnp.zeros(r.misc.shape[1:], F32)
    r.misc[d, 0:1, 0:R] = r.s_ga[...]
    r.misc[d, 1:2, 0:R] = r.s_gf[...]
    r.misc[d, 2 : 2 + heads, 0:BR] = r.s_bt[...]
    load_o.wait()
    r.wo_all[t, d] = r.s_attn[3].astype(BF)
    all_here()
    g_misc.start()
    g_a.start()
    g_o.start()
    for n, (load, ref, g) in enumerate(zip(load_f, (r.wg, r.wu, r.wd), g_ffn)):
        load.wait()
        ref[d] = r.s_ffn[n].astype(BF)
        g.start()
    load_b.wait()
    load_p.wait()

    def split_bucket(i, carry):
        rows = rows_of(i, SUB)
        ids = r.buckets[rows, :]
        r.high[rows, :] = (ids // LOW).astype(BF)
        r.low[rows, :] = (ids % LOW).astype(BF)
        return carry

    lax.fori_loop(0, T // SUB, split_bucket, 0)
    g_misc.forward()
    g_a.forward()
    g_misc.finish()
    gains = jnp.concatenate([r.misc[n, :, 0:R] for n in range(dp)], axis=1).astype(BF).astype(F32)
    gain_attn, gain_ffn = gains[0:1], gains[1:2]
    lane = lax.broadcasted_iota(jnp.int32, (8, LANES), 1)
    table = jnp.zeros((8, LANES), F32)
    for n in range(dp):
        moved = r.misc[n] if n == 0 else pltpu.roll(r.misc[n], n * BR, 1)
        table = jnp.where(lane // BR == n, moved, table)
    table = table.astype(BF).astype(F32)[2 : 2 + heads]
    real = r.pad[...] > 0

    def fill_bias(i, carry):
        rows = rows_of(i, SUB)
        ids = r.buckets[rows, :]
        for h in range(heads):
            bias = lookup(jnp.broadcast_to(table[h : h + 1, :], (SUB, LANES)), ids)
            r.ds[h, rows, :] = jnp.where(real, bias, masked_score).astype(BF)
        return carry

    lax.fori_loop(0, T // SUB // 2, fill_bias, 0)
    g_o.forward()
    g_ffn[0].step(1)
    lax.fori_loop(T // SUB // 2, T // SUB, fill_bias, 0)
    g_ffn[1].step(1)
    load_x.wait()
    load_g.wait()

    g_a.finish()

    def project(b, carry):
        rows = rows_of(b, BLOCK)
        x = r.x[rows, :].astype(F32)
        n1 = (x * inverse_rms(x) * gain_attn).astype(BF)
        r.n1[rows, :] = n1
        made = dot(n1, r.wa[...].reshape(D, I3), NN).astype(BF)
        for n, out in enumerate((r.q, r.k, r.v)):
            for h in range(heads):
                out[h, rows, :] = made[:, n * I + h * HD : n * I + (h + 1) * HD]
        return carry

    lax.fori_loop(0, NB, project, 0)
    g_ffn[2].step(1)
    g_o.finish()
    s_wo.start()

    def mix(b):
        rows = slice(b * BLOCK, (b + 1) * BLOCK)
        return [dot(r.p[h, rows, :], r.v[h], NN) for h in range(heads)]

    def put_mix(b, mixed):
        rows = slice(b * BLOCK, (b + 1) * BLOCK)
        for h in range(heads):
            r.o[h, rows, :] = mixed[h]
        r.o_all[t, rows, :] = jnp.concatenate([m.astype(BF) for m in mixed], axis=1)
        s_mix[b].start()

    for b in range(NB):
        rows = slice(b * BLOCK, (b + 1) * BLOCK)
        mixed = mix(b - 1) if b > 0 else None
        weights = []
        for h in range(heads):
            scores = dot(r.q[h, rows, :], r.k[h], NT) + r.ds[h, rows, :].astype(F32)
            top = jnp.max(scores, axis=1, keepdims=True)
            e = jnp.exp(scores - top)
            weights.append((e * (1.0 / jnp.sum(e, axis=1, keepdims=True))).astype(BF))
        for h in range(heads):
            r.p[h, rows, :] = weights[h]
        if b > 0:
            put_mix(b - 1, mixed)
        if b == 0:
            g_ffn[0].step(2)
            g_ffn[1].step(2)
        if b == 1:
            g_ffn[2].step(2)
            s_wo.forward()
        if b == 2:
            g_ffn[0].step(3)
            s_mix[0].forward()
    put_mix(NB - 1, mix(NB - 1))
    g_ffn[1].step(3)
    s_mix[1].forward()
    g_ffn[2].step(3)
    s_mix[2].forward()
    s_wo.finish()
    for n in range(NT_):
        r.wo_cat[:, n * I : (n + 1) * I] = r.wo_all[n].reshape(D, I)
    g_ffn[0].step(4)
    s_mix[3].forward()
    g_ffn[1].step(4)
    for step in range(5, dp // 2 + 1):
        for g in g_ffn:
            g.step(step - 1 if g is g_ffn[2] else step)

    def halves_of(b):
        halves = [rows_of(2 * b + 1 - c, half), rows_of(2 * b + c, half)]

        def both(ref):
            return jnp.concatenate([ref[rows, :] for rows in halves], axis=0)

        def put(ref, values):
            ref[halves[0], :] = values[:half]
            ref[halves[1], :] = values[half:]

        return halves, both, put

    def feed(b):
        s_mix[b].finish()
        halves, both, put = halves_of(b)
        mixed = jnp.concatenate(
            [
                jnp.concatenate([r.o_all[n, rows, :] for n in range(NT_)], axis=1)
                for rows in halves
            ],
            axis=0,
        )
        middle = both(r.x).astype(F32) + dot(mixed, r.wo_cat[...], NT)
        r.mid[b] = middle[half:]
        n2 = (middle * inverse_rms(middle) * gain_ffn).astype(BF)
        put(r.n2, n2)
        w_gate, w_up = [w[...].reshape(D, F) for w in (r.wg, r.wu)]
        gate = dot(n2, w_gate, NN)
        up = dot(n2, w_up, NN)
        square = gate * gate
        th = jnp.tanh(gelu_scale * gate * (1.0 + gelu_cube * square))
        left = 0.5 * (1.0 + th)
        active = gate * left
        slope = left + 0.5 * gate * (1.0 - th * th) * (
            gelu_scale * (1.0 + 3.0 * gelu_cube * square)
        )
        hidden = (active * up).astype(BF)
        put(r.hidden, hidden)
        return hidden, up, active, slope

    def feed_back(b, hidden, up, active, slope):
        halves, both, put = halves_of(b)
        w_gate, w_up, w_down = [w[...].reshape(D, F) for w in (r.wg, r.wu, r.wd)]
        dhidden = dot(both(r.g), w_down, NN)
        dgate = (dhidden * up * slope).astype(BF)
        dup = (dhidden * active).astype(BF)
        put(r.dgate, dgate)
        put(r.dup, dup)
        h_mid[b].start(dot(dgate, w_gate, NT) + dot(dup, w_up, NT))
        h_out[b].start(dot(hidden, w_down, NT))

    def to_middle(b):
        rows = rows_of(2 * b + c, half)
        dn2 = h_mid[b].finish()
        dmiddle = r.g[rows, :].astype(F32) + norm_back(dn2, r.mid[b], gain_ffn)
        r.dmid[b] = dmiddle
        r.dmb[rows, :] = dmiddle.astype(BF)
        ref = r.dmb.at[rows]
        comm.send(ref, ref, partner, p_dmb[b])

    def scatter_grad(name, values):
        part = getattr(r, "part_" + name)
        part[...] = values.astype(BF).reshape(part.shape)
        sc[name].start()

    w_out = r.wo_all[t].reshape(D, I)

    def back(b):
        comm.arrived(r.dmb.at[rows_of(2 * b + 1 - c, half)], partner, p_dmb[b])
        rows = slice(b * BLOCK, (b + 1) * BLOCK)
        do = dot(r.dmb[rows, :], w_out, NN).astype(BF)
        made = []
        for h in range(heads):
            do_h = do[:, h * HD : (h + 1) * HD]
            p = r.p[h, rows, :]
            delta = jnp.sum(do_h.astype(F32) * r.o[h, rows, :], axis=1, keepdims=True)
            ds = (p.astype(F32) * (dot(do_h, r.v[h], NT) - delta)).astype(BF)
            r.ds[h, rows, :] = ds
            made.append(dot(ds, r.k[h], NN).astype(BF))
            more_k, more_v = dot(ds, r.q[h, rows, :], TN), dot(p, do_h, TN)
            if b > 0:
                more_k, more_v = r.dk[h] + more_k, r.dv[h] + more_v
            r.dk[h], r.dv[h] = more_k, more_v
        r.da[rows, 0:I] = jnp.concatenate(made, axis=1)
        more = dot(r.dmb[rows, :], r.o_all[t, rows, :], TN)
        r.go[...] = more if b == 0 else r.go[...] + more

    for b in range(NB):
        made = feed(b)
        if b == 0:
            g_ffn[2].step(dp // 2)
        feed_back(b, *made)
        if b >= 1:
            h_mid[b - 1].middle()
    scatter_grad("d", dot(r.g[...], r.hidden[...], TN))
    h_mid[NB - 1].middle()
    scatter_grad("g", dot(r.n2[...], r.dgate[...], TN))
    to_middle(0)
    scatter_grad("u", dot(r.n2[...], r.dup[...], TN))
    for b in range(1, NB):
        to_middle(b)
        back(b - 1)
        if b == 2:
            sc["d"].middle()
    h_out[0].middle()
    back(NB - 1)
    r.da[:, I : 2 * I] = jnp.concatenate([r.dk[h].astype(BF) for h in range(heads)], axis=1)
    r.da[:, 2 * I : I3] = jnp.concatenate([r.dv[h].astype(BF) for h in range(heads)], axis=1)

    for b in range(NB):
        halves = [rows_of(2 * b + 1 - c, half), rows_of(2 * b + c, half)]
        former = jnp.concatenate([r.da[rows, :] for rows in halves], axis=0)
        h_in[b].start(dot(former, r.wa[...].reshape(D, I3), NT))
        if b >= 1:
            h_in[b - 1].middle()
    scatter_grad("a", dot(r.n1[...], r.da[...], TN))
    h_in[NB - 1].middle()
    scatter_grad("o", r.go[...])
    sc["g"].middle()
    for b in range(1, NB):
        h_out[b].middle()

    def bias_rows(i, carry):
        former, latter = [], []
        for g in range(GROUPS):
            rows = rows_of(i * GROUPS + g, GROUP)
            high, low = r.high[rows, :], r.low[rows, :]
            one, zero = jnp.ones_like(high), jnp.zeros_like(high)
            former.append(
                jnp.concatenate(
                    [jnp.where(high == BF(n), one, zero) for n in range(BUCKETS // LOW)], axis=0
                )
            )
            part = []
            for n in range(LOW):
                match = low == BF(n)
                part += [jnp.where(match, r.ds[h, rows, :], zero) for h in range(heads)]
            latter.append(jnp.concatenate(part, axis=0))
        return carry + dot(
            jnp.concatenate(former, axis=1), jnp.concatenate(latter, axis=1), NT
        )

    count = T // (GROUP * GROUPS)
    sums = lax.fori_loop(0, count // 2, bias_rows, jnp.zeros(r.bias_sum.shape, F32))
    r.bias_sum[...] = sums
    sc["a"].middle()
    sc["u"].middle()
    sums = r.bias_sum[...]
    sums = lax.fori_loop(count // 2, count, bias_rows, sums)
    tall, wide = r.bias_sum.shape
    row = lax.broadcasted_iota(jnp.int32, (tall, wide), 0)
    column = lax.broadcasted_iota(jnp.int32, (tall, wide), 1)
    sums = jnp.where(row % GROUP == column % GROUP, sums, 0.0)
    sums = jnp.sum(sums.reshape(BUCKETS // LOW, GROUP, wide), axis=1)
    bucket = lax.broadcasted_iota(jnp.int32, (LANES, BUCKETS // LOW), 0)
    high = lax.broadcasted_iota(jnp.int32, (LANES, BUCKETS // LOW), 1)
    spread = jnp.where(bucket // LOW == high, 1.0, 0.0)
    spread = dot(spread.astype(BF), sums.astype(BF), NN)
    bucket = lax.broadcasted_iota(jnp.int32, (LANES, wide), 0)
    column = lax.broadcasted_iota(jnp.int32, (LANES, wide), 1)
    spread = jnp.where(bucket % LOW == column // (heads * GROUP), spread, 0.0)
    head = lax.broadcasted_iota(jnp.int32, (8, wide), 0)
    column = lax.broadcasted_iota(jnp.int32, (8, wide), 1)
    of_head = jnp.where(column // GROUP % heads == head, 1.0, 0.0)
    by_head = dot(of_head.astype(BF), spread.astype(BF), NT)
    for n in range(dp):
        moved = by_head if n == 0 else pltpu.roll(by_head, LANES - n * BR, 1)
        r.part_m[n // comm.Y, n % comm.Y] = moved
    sc["m"].start()
    sc["o"].middle()

    stores = []
    for b in range(NB):
        rows = rows_of(2 * b + c, half)
        x = r.x[rows, :].astype(F32)
        total = r.dmid[b] + norm_back(h_in[b].finish(), x, gain_attn)
        r.s_ig[b] = total.astype(BF)
        ref = r.input_grad.at[rows]
        comm.send(r.s_ig.at[b], ref, partner, p_ig[b])
        stores.append(local(r.s_ig.at[b], ref))
        stores[-1].start()
        if b == 0:
            sc["m"].middle()

    outs = {}

    def keep(name, value, out):
        ref = getattr(r, "s_" + name)
        ref[...] = value
        stores.append(local(ref, out))
        stores[-1].start()

    for n, out in zip("dgu", (r.o_d, r.o_g, r.o_u)):
        outs[n] = sc[n].finish()
        keep(n, outs[n], out)
    outs["a"] = sc["a"].finish()
    for n, name, out in zip(range(3), "qkv", (r.o_q, r.o_k, r.o_v)):
        keep(name, outs["a"][:, n * I : (n + 1) * I], out)

    def gain_grad(pairs, gain):
        total = jnp.zeros((8, R), F32)
        for weight, grad in pairs:
            product = weight.astype(F32) * grad
            total = total + dot(
                jnp.ones((8, product.shape[1]), F32), product, NT, precision=lax.Precision.HIGHEST
            )
        return total[0:1] / gain.astype(BF).astype(F32)

    r.norm[t] = jnp.zeros(r.norm.shape[1:], F32)
    r.norm[t, 0:1, 0:R] = gain_grad([(r.wa[d], outs["a"])], r.s_ga[...])
    r.norm[t, 1:2, 0:R] = gain_grad([(r.wg[d], outs["g"]), (r.wu[d], outs["u"])], r.s_gf[...])
    for n in range(1, NT_):
        ref = r.norm.at[t]
        comm.send(ref, ref, (d, (t + n) % NT_), p_norm[n])
    keep("o", sc["o"].finish(), r.o_o)
    keep("m", sc["m"].finish()[0:heads, 0:BR], r.o_m)
    for b in range(NB):
        rows = rows_of(2 * b + c, half)
        total = h_out[b].finish() + r.mid[b]
        r.s_bo[b] = total.astype(BF)
        ref = r.block_out.at[rows]
        comm.send(r.s_bo.at[b], ref, partner, p_bo[b])
        stores.append(local(r.s_bo.at[b], ref))
        stores[-1].start()
    for n in range(1, NT_):
        comm.arrived(r.norm.at[(t - n) % NT_], (d, (t + n) % NT_), p_norm[n])
    total = r.norm[0]
    for n in range(1, NT_):
        total = total + r.norm[n]
    keep("na", total[0:1, 0:R], r.o_na)
    keep("nf", total[1:2, 0:R], r.o_nf)
    for b in range(NB):
        rows = rows_of(2 * b + 1 - c, half)
        comm.arrived(r.block_out.at[rows], partner, p_bo[b])
        comm.arrived(r.input_grad.at[rows], partner, p_ig[b])
    comm.drain()
    for store in stores:
        store.wait()


def hand_over(names, pieces, *refs):
    count = len(names)
    before, after, held = [dict(zip(names, refs[n * count : (n + 1) * count])) for n in range(3)]
    wide, sems = refs[3 * count :]
    sem_at = iter(range(4 * (count + 2 * pieces)))

    def parts(name):
        rows = before[name].shape[0]
        step = rows // pieces if name in ("block_out", "input_grad") else rows
        return [slice(k, k + step) for k in range(0, rows, step)]

    jobs = []
    order = ["input_grad", "block_out"] + [n for n in names if n not in ("input_grad", "block_out")]
    for name in order:
        for rows in parts(name):
            copy = pltpu.make_async_copy(
                before[name].at[rows], held[name].at[rows], sems.at[next(sem_at)]
            )
            copy.start()
            jobs.append((name, rows, copy))
    stores = []
    for name, rows, copy in jobs:
        copy.wait()
        source = held[name]
        if name == "input_grad":
            wide[rows, :] = source[rows, :].astype(F32)
            source = wide
        stores.append(
            pltpu.make_async_copy(source.at[rows], after[name].at[rows], sems.at[next(sem_at)])
        )
        stores[-1].start()
    for store in stores:
        store.wait()


def per_device(
    sizes,
    tokens,
    cotangent,
    w_query,
    w_key,
    w_value,
    w_out,
    w_gate,
    w_up,
    w_down,
    norm_attn,
    norm_ffn,
    bias_table,
    buckets,
    padding,
):
    T, D = tokens.shape
    R, I = w_query.shape
    F = w_gate.shape[1]
    BR, heads = bias_table.shape
    HD = I // heads
    Z, Y, X = sizes
    dp, tensor = Z * Y, 2 * X
    NB, half = T // BLOCK, BLOCK // 2
    S, V = jax.ShapeDtypeStruct, pltpu.VMEM
    inputs = dict(
        x_in=tokens,
        g_in=cotangent,
        wq_in=w_query,
        wk_in=w_key,
        wv_in=w_value,
        wo_in=w_out.T,
        wg_in=w_gate,
        wu_in=w_up,
        wd_in=w_down.T,
        ga_in=norm_attn.reshape(1, R),
        gf_in=norm_ffn.reshape(1, R),
        bt_in=bias_table.T,
        bucket_in=buckets,
        pad_in=padding,
    )
    outputs = dict(
        block_out=S((T, D), BF),
        input_grad=S((T, D), BF),
        o_q=S((R, I), F32),
        o_k=S((R, I), F32),
        o_v=S((R, I), F32),
        o_o=S((R, I), F32),
        o_g=S((R, F), F32),
        o_u=S((R, F), F32),
        o_d=S((R, F), F32),
        o_na=S((1, R), F32),
        o_nf=S((1, R), F32),
        o_m=S((heads, BR), F32),
    )
    scratch = dict(
        s_attn=V((4, R, I), F32),
        s_ffn=V((3, R, F), F32),
        s_ga=V((1, R), F32),
        s_gf=V((1, R), F32),
        s_bt=V((heads, BR), F32),
        x=V((T, D), BF),
        g=V((T, D), BF),
        buckets=V((T, T), jnp.int32),
        pad=V((1, T), jnp.int32),
        misc=V((dp, 8, LANES), F32),
        wa=V((dp, R, 3 * I), BF),
        high=V((T, T), BF),
        low=V((T, T), BF),
        wo_all=V((tensor, dp, R, I), BF),
        wo_cat=V((D, tensor * I), BF),
        wg=V((dp, R, F), BF),
        wu=V((dp, R, F), BF),
        wd=V((dp, R, F), BF),
        n1=V((T, D), BF),
        q=V((heads, T, HD), BF),
        k=V((heads, T, HD), BF),
        v=V((heads, T, HD), BF),
        p=V((heads, T, T), BF),
        o=V((heads, T, HD), F32),
        o_all=V((tensor, T, I), BF),
        mid=V((NB, half, D), F32),
        n2=V((T, D), BF),
        hidden=V((T, F), BF),
        dgate=V((T, F), BF),
        dup=V((T, F), BF),
        m_away=V((NB, half, D), BF),
        m_kept=V((NB, half, D), F32),
        m_near=V((NB, half, D), BF),
        m_far=V((X, NB, half, D), BF),
        f_away=V((NB, half, D), BF),
        f_kept=V((NB, half, D), F32),
        f_near=V((NB, half, D), BF),
        f_far=V((X, NB, half, D), BF),
        dmid=V((NB, half, D), F32),
        dmb=V((T, D), BF),
        i_away=V((NB, half, D), BF),
        i_kept=V((NB, half, D), F32),
        i_near=V((NB, half, D), BF),
        i_far=V((X, NB, half, D), BF),
        dk=V((heads, T, HD), F32),
        dv=V((heads, T, HD), F32),
        da=V((T, 3 * I), BF),
        go=V((D, I), F32),
        ds=V((heads, T, T), BF),
        bias_sum=V((BUCKETS // LOW * GROUP, LOW * heads * GROUP), F32),
        s_bo=V((NB, half, D), BF),
        s_ig=V((NB, half, D), BF),
        norm=V((tensor, 8, LANES), F32),
        s_m=V((heads, BR), F32),
        s_na=V((1, R), F32),
        s_nf=V((1, R), F32),
    )
    widths = dict(a=3 * I, o=I, g=F, u=F, d=F)
    for n, width in widths.items():
        scratch["part_" + n] = V((Z, Y, R, width), BF)
        scratch["fy_" + n] = V((Y - 1, Z, R, width), BF)
        scratch["mine_" + n] = V((Z, R, width), BF)
        scratch["fz_" + n] = V((Z - 1, R, width), BF)
    for n, width in dict(q=I, k=I, v=I, o=I, g=F, u=F, d=F).items():
        scratch["s_" + n] = V((R, width), F32)
    scratch["part_m"] = V((Z, Y, 8, LANES), F32)
    scratch["fy_m"] = V((Y - 1, Z, 8, LANES), F32)
    scratch["mine_m"] = V((Z, 8, LANES), F32)
    scratch["fz_m"] = V((Z - 1, 8, LANES), F32)
    count = 3 * (Z - 1 + Z * (Y - 1)) + 3 * (dp - 1) + (1 + NB) * (2 * X - 1)
    count += 3 * NB * X + 3 * NB + tensor - 1 + 6 * (Y + Z - 2)
    scratch["local_sems"] = pltpu.SemaphoreType.DMA((14 + 2 * NB + 10,))
    scratch["sems"] = pltpu.SemaphoreType.DMA((2 * count,))
    names = [*inputs, *outputs, *scratch]
    made = pl.pallas_call(
        functools.partial(layer_kernel, sizes, heads, names),
        out_shape=list(outputs.values()),
        in_specs=[pl.BlockSpec(memory_space=pl.ANY)] * len(inputs),
        out_specs=[pl.BlockSpec(memory_space=pl.ANY)] * len(outputs),
        scratch_shapes=list(scratch.values()),
        compiler_params=pltpu.CompilerParams(
            collective_id=0, has_side_effects=True, vmem_limit_bytes=62 << 20
        ),
        name="layer",
    )(*inputs.values())
    final = {**outputs, "input_grad": S((T, D), F32)}
    pieces = 4
    made = pl.pallas_call(
        functools.partial(hand_over, list(outputs), pieces),
        out_shape=list(final.values()),
        in_specs=[pl.BlockSpec(memory_space=pl.ANY)] * len(outputs),
        out_specs=[pl.BlockSpec(memory_space=pl.ANY)] * len(outputs),
        scratch_shapes=[V(o.shape, o.dtype) for o in outputs.values()]
        + [V((T, D), F32), pltpu.SemaphoreType.DMA((4 * (len(outputs) + 2 * pieces),))],
        name="hand_over",
    )(*made)
    out = dict(zip(outputs, made))
    return (
        out["block_out"],
        out["input_grad"],
        out["o_q"],
        out["o_k"],
        out["o_v"],
        out["o_o"].T,
        out["o_g"],
        out["o_u"],
        out["o_d"].T,
        out["o_na"].reshape(R),
        out["o_nf"].reshape(R),
        out["o_m"].T,
    )


def solution(mesh):
    shards, halves = mesh.shape["dp"], mesh.shape["tensor"]
    X = halves // 2
    Y = X if shards % X == 0 else 1
    sizes = (shards // Y, Y, X)
    in_specs = (
        P("dp", None),
        P("dp", None),
        P("dp", "tensor"),
        P("dp", "tensor"),
        P("dp", "tensor"),
        P("tensor", "dp"),
        P("dp", "tensor"),
        P("dp", "tensor"),
        P("tensor", "dp"),
        P("dp"),
        P("dp"),
        P("dp", "tensor"),
        P(),
        P("dp", None),
    )
    out_specs = (
        P("dp", None),
        P("dp", None),
        P("dp", "tensor"),
        P("dp", "tensor"),
        P("dp", "tensor"),
        P("tensor", "dp"),
        P("dp", "tensor"),
        P("dp", "tensor"),
        P("tensor", "dp"),
        P("dp"),
        P("dp"),
        P("dp", "tensor"),
    )
    return jax.shard_map(
        functools.partial(per_device, sizes),
        mesh=mesh,
        in_specs=in_specs,
        out_specs=out_specs,
        check_vma=False,
    )
```

```python
import functools
import types

import jax
import jax.numpy as jnp
from jax import lax
from jax.experimental import pallas as pl
from jax.experimental.pallas import tpu as pltpu
from jax.sharding import PartitionSpec as P

MESH = pl.DeviceIdType.MESH
BF = jnp.bfloat16
F32 = jnp.float32
NN = (((1,), (0,)), ((), ()))
NT = (((1,), (1,)), ((), ()))
TN = (((0,), (0,)), ((), ()))
epsilon = 1e-06
masked_score = -1000000000.0
LANES = 128
BUCKETS = 32
LOW = 4
GROUP = 32
BLOCK = 256
SUB = 128
GROUPS = 8
gelu_scale = 0.7978845608028654
gelu_cube = 0.044715


def dot(former, latter, dims, **more):
    return lax.dot_general(former, latter, dims, preferred_element_type=F32, **more)


def rows_of(index, size):
    return pl.ds(pl.multiple_of(index * size, size), size)


def lookup(table, ids):
    tiles = ids.shape[1] // LANES
    return jnp.concatenate(
        [
            jnp.take_along_axis(table, ids[:, c * LANES : (c + 1) * LANES], axis=1)
            for c in range(tiles)
        ],
        axis=1,
    )


def inverse_rms(values):
    return lax.rsqrt(jnp.mean(values * values, axis=1, keepdims=True) + epsilon)


def norm_back(grad_normed, values, gain):
    r = inverse_rms(values)
    u = grad_normed * gain
    return r * u - values * (r * r * r) * jnp.mean(u * values, axis=1, keepdims=True)


class Comm:
    def __init__(self, sizes, sems):
        self.Z, self.Y, self.X = sizes
        self.sems = sems
        self.used = 0
        self.d, self.t = lax.axis_index("dp"), lax.axis_index("tensor")
        self.z, self.y = self.d // self.Y, self.d % self.Y
        self.x, self.c = self.t // 2, self.t % 2
        self.place = self.y * self.Z + self.z + (self.y % 2) * (self.Z - 1 - 2 * self.z)
        self.pending = []

    def z_peer(self, k):
        return ((self.z + k) % self.Z) * self.Y + self.y, self.t

    def y_peer(self, j):
        return self.z * self.Y + (self.y + j) % self.Y, self.t

    def x_to(self, j, other=0):
        core = self.c if other == 0 else 1 - self.c
        return ((self.x + j) % self.X) * 2 + core

    def x_from(self, j, other=0):
        core = self.c if other == 0 else 1 - self.c
        return ((self.x - j) % self.X) * 2 + core

    def origin(self, kz, j=0):
        return ((self.z - kz) % self.Z) * self.Y + (self.y - j) % self.Y

    def ring(self, place):
        count = self.Z * self.Y
        place = (place + count) % count
        y, z = place // self.Z, place % self.Z
        return (z + (y % 2) * (self.Z - 1 - 2 * z)) * self.Y + y

    def pair(self):
        self.used += 2
        return self.sems.at[self.used - 2], self.sems.at[self.used - 1]

    def barrier(self):
        peers = [self.z_peer(k) for k in range(1, self.Z)]
        peers += [self.y_peer(j) for j in range(1, self.Y)]
        peers += [(self.d, self.x_to(j)) for j in range(1, self.X)]
        peers += [(self.d, self.x_to(j, 1)) for j in range(self.X)]
        peers += [(self.ring(self.place + n), self.t) for n in (1, -1)]
        semaphore = pltpu.get_barrier_semaphore()
        for peer in peers:
            pl.semaphore_signal(semaphore, inc=1, device_id=peer, device_id_type=MESH)
        return lambda: pl.semaphore_wait(semaphore, len(peers))

    def copy(self, src, dst, peer, pair):
        return pltpu.make_async_remote_copy(
            src_ref=src,
            dst_ref=dst,
            send_sem=pair[0],
            recv_sem=pair[1],
            device_id=peer,
            device_id_type=MESH,
        )

    def send(self, src, dst, peer, pair):
        made = self.copy(src, dst, peer, pair)
        made.start()
        self.pending.append(made)

    def arrived(self, ref, peer, pair):
        self.copy(ref, ref, peer, pair).wait_recv()

    def drain(self):
        for made in self.pending:
            made.wait_send()
        self.pending = []


class Gather:
    def __init__(self, comm, full):
        self.comm, self.full = comm, full
        Z, Y = comm.Z, comm.Y
        self.zp = {k: comm.pair() for k in range(1, Z)}
        self.yp = {(k, j): comm.pair() for k in range(Z) for j in range(1, Y)}

    def send_y(self, k):
        m = self.comm
        block = self.full.at[m.origin(k)]
        for j in range(1, m.Y):
            m.send(block, block, m.y_peer(j), self.yp[k, j])

    def start(self):
        m = self.comm
        own = self.full.at[m.d]
        for k in range(m.Z - 1, 0, -1):
            m.send(own, own, m.z_peer(k), self.zp[k])
        self.send_y(0)

    def forward(self):
        m = self.comm
        for k in range(1, m.Z):
            m.arrived(self.full.at[m.origin(k)], m.z_peer(k), self.zp[k])
            self.send_y(k)

    def finish(self):
        m = self.comm
        for k in range(m.Z):
            for j in range(1, m.Y):
                m.arrived(self.full.at[m.origin(k, j)], m.y_peer(j), self.yp[k, j])


class Ring:
    def __init__(self, comm, full, turn):
        self.comm, self.full = comm, full
        count = comm.Z * comm.Y
        most, least = count // 2, count - 1 - count // 2
        self.reach = (most, least) if turn == 0 else (least, most)
        self.pairs = [[comm.pair() for _ in range(n)] for n in self.reach]

    def block(self, way, step):
        m = self.comm
        return self.full.at[m.ring(m.place - step if way == 0 else m.place + step)]

    def pass_on(self, way, step):
        m = self.comm
        if step < self.reach[way]:
            ref = self.block(way, step)
            peer = m.ring(m.place + 1 if way == 0 else m.place - 1), m.t
            m.send(ref, ref, peer, self.pairs[way][step])

    def start(self):
        for way in range(2):
            self.pass_on(way, 0)

    def step(self, step):
        m = self.comm
        for way in range(2):
            if step <= self.reach[way]:
                peer = m.ring(m.place + 1 if way == 0 else m.place - 1), m.t
                m.arrived(self.block(way, step), peer, self.pairs[way][step - 1])
                self.pass_on(way, step)


class Share:
    def __init__(self, comm, part):
        self.comm, self.part = comm, part
        self.xp = {j: comm.pair() for j in range(1, comm.X)}
        self.cp = {j: comm.pair() for j in range(comm.X)}

    def send_core(self, j):
        m = self.comm
        ref = self.part(m.x_from(j))
        m.send(ref, ref, (m.d, m.x_to(0, 1)), self.cp[j])

    def start(self):
        m = self.comm
        ref = self.part(m.t)
        for j in range(1, m.X):
            m.send(ref, ref, (m.d, m.x_to(j)), self.xp[j])
        self.send_core(0)

    def forward(self):
        m = self.comm
        for j in range(1, m.X):
            m.arrived(self.part(m.x_from(j)), (m.d, m.x_to(j)), self.xp[j])
            self.send_core(j)

    def finish(self):
        m = self.comm
        for j in range(m.X):
            m.arrived(self.part(m.x_from(j, 1)), (m.d, m.x_to(0, 1)), self.cp[j])


class Scatter:
    def __init__(self, comm, part, from_y, mine, from_z):
        self.comm, self.part, self.from_y, self.mine, self.from_z = comm, part, from_y, mine, from_z
        self.yp = {j: comm.pair() for j in range(1, comm.Y)}
        self.zp = {k: comm.pair() for k in range(1, comm.Z)}

    def start(self):
        m = self.comm
        for j in range(1, m.Y):
            src = self.part.at[:, (m.y + j) % m.Y]
            m.send(src, self.from_y.at[j - 1], m.y_peer(j), self.yp[j])

    def middle(self):
        m = self.comm
        for j in range(1, m.Y):
            m.arrived(self.from_y.at[j - 1], m.y_peer(j), self.yp[j])
        total = self.part[:, m.y].astype(F32)
        for j in range(1, m.Y):
            total = total + self.from_y[j - 1].astype(F32)
        self.mine[...] = total.astype(self.mine.dtype)
        for k in range(1, m.Z):
            m.send(self.mine.at[(m.z + k) % m.Z], self.from_z.at[k - 1], m.z_peer(k), self.zp[k])

    def finish(self):
        m = self.comm
        total = self.mine[m.z].astype(F32)
        for k in range(1, m.Z):
            m.arrived(self.from_z.at[k - 1], m.z_peer(k), self.zp[k])
            total = total + self.from_z[k - 1].astype(F32)
        return total


class Halves:
    def __init__(self, comm, block, away, kept, near, far):
        self.comm, self.block = comm, block
        self.away, self.kept, self.near, self.far = away, kept, near, far
        self.cp = comm.pair()
        self.xp = {j: comm.pair() for j in range(1, comm.X)}

    def start(self, values):
        m, b = self.comm, self.block
        half = BLOCK // 2
        self.away[b] = values[:half].astype(BF)
        self.kept[b] = values[half:]
        m.send(self.away.at[b], self.near.at[b], (m.d, m.x_to(0, 1)), self.cp)

    def middle(self):
        m, b = self.comm, self.block
        m.arrived(self.near.at[b], (m.d, m.x_to(0, 1)), self.cp)
        self.far[m.x, b] = (self.kept[b] + self.near[b].astype(F32)).astype(BF)
        for j in range(1, m.X):
            ref = self.far.at[m.x, b]
            m.send(ref, ref, (m.d, m.x_to(j)), self.xp[j])

    def finish(self):
        m, b = self.comm, self.block
        for j in range(1, m.X):
            m.arrived(self.far.at[(m.x - j) % m.X, b], (m.d, m.x_to(j)), self.xp[j])
        total = self.far[0, b].astype(F32)
        for j in range(1, m.X):
            total = total + self.far[j, b].astype(F32)
        return total


def layer_kernel(sizes, heads, names, *refs):
    r = types.SimpleNamespace(**dict(zip(names, refs)))
    T, D = r.x.shape
    dp, R, I3 = r.wa.shape
    I, F = r.wo_all.shape[3], r.wg.shape[2]
    NT_ = r.wo_all.shape[0]
    BR = BUCKETS // dp
    HD = I // heads
    NB = T // BLOCK
    half = BLOCK // 2
    sem_at = iter(range(1000))

    def local(src, dst):
        return pltpu.make_async_copy(src, dst, r.local_sems.at[next(sem_at)])

    early = [
        local(r.wq_in, r.s_attn.at[0]),
        local(r.wk_in, r.s_attn.at[1]),
        local(r.wv_in, r.s_attn.at[2]),
        local(r.ga_in, r.s_ga),
        local(r.gf_in, r.s_gf),
        local(r.bt_in, r.s_bt),
    ]
    load_o = local(r.wo_in, r.s_attn.at[3])
    load_f = [local(ref, r.s_ffn.at[n]) for n, ref in enumerate((r.wg_in, r.wu_in, r.wd_in))]
    load_b = local(r.bucket_in, r.buckets)
    load_p = local(r.pad_in, r.pad)
    load_x = local(r.x_in, r.x)
    load_g = local(r.g_in, r.g)
    for load in early + [load_o] + load_f + [load_b, load_p, load_x, load_g]:
        load.start()
    comm = Comm(sizes, r.sems)
    all_here = comm.barrier()
    d, t, c = comm.d, comm.t, comm.c
    partner = (d, comm.x_to(0, 1))
    g_misc, g_a, g_o = [Gather(comm, f) for f in (r.misc, r.wa, r.wo_all.at[t])]
    g_ffn = [Ring(comm, f, n % 2) for n, f in enumerate((r.wg, r.wu, r.wd))]
    s_wo = Share(comm, lambda n: r.wo_all.at[n])
    s_mix = [Share(comm, lambda n, b=b: r.o_all.at[n, rows_of(b, BLOCK)]) for b in range(NB)]
    h_mid = [Halves(comm, b, r.m_away, r.m_kept, r.m_near, r.m_far) for b in range(NB)]
    h_out = [Halves(comm, b, r.f_away, r.f_kept, r.f_near, r.f_far) for b in range(NB)]
    h_in = [Halves(comm, b, r.i_away, r.i_kept, r.i_near, r.i_far) for b in range(NB)]
    p_dmb = [comm.pair() for _ in range(NB)]
    p_bo = [comm.pair() for _ in range(NB)]
    p_ig = [comm.pair() for _ in range(NB)]
    p_norm = {n: comm.pair() for n in range(1, NT_)}
    sc = {
        n: Scatter(comm, *[getattr(r, f"{kind}_{n}") for kind in ("part", "fy", "mine", "fz")])
        for n in "aogudm"
    }

    for load in early:
        load.wait()
    for n in range(3):
        r.wa[d, :, n * I : (n + 1) * I] = r.s_attn[n].astype(BF)
    r.misc[d] = jnp.zeros(r.misc.shape[1:], F32)
    r.misc[d, 0:1, 0:R] = r.s_ga[...]
    r.misc[d, 1:2, 0:R] = r.s_gf[...]
    r.misc[d, 2 : 2 + heads, 0:BR] = r.s_bt[...]
    load_o.wait()
    r.wo_all[t, d] = r.s_attn[3].astype(BF)
    all_here()
    g_misc.start()
    g_a.start()
    g_o.start()
    for n, (load, ref, g) in enumerate(zip(load_f, (r.wg, r.wu, r.wd), g_ffn)):
        load.wait()
        ref[d] = r.s_ffn[n].astype(BF)
        g.start()
    load_b.wait()
    load_p.wait()

    def split_bucket(i, carry):
        rows = rows_of(i, SUB)
        ids = r.buckets[rows, :]
        r.high[rows, :] = (ids // LOW).astype(BF)
        r.low[rows, :] = (ids % LOW).astype(BF)
        return carry

    lax.fori_loop(0, T // SUB, split_bucket, 0)
    g_misc.forward()
    g_a.forward()
    g_misc.finish()
    gains = jnp.concatenate([r.misc[n, :, 0:R] for n in range(dp)], axis=1).astype(BF).astype(F32)
    gain_attn, gain_ffn = gains[0:1], gains[1:2]
    lane = lax.broadcasted_iota(jnp.int32, (8, LANES), 1)
    table = jnp.zeros((8, LANES), F32)
    for n in range(dp):
        moved = r.misc[n] if n == 0 else pltpu.roll(r.misc[n], n * BR, 1)
        table = jnp.where(lane // BR == n, moved, table)
    table = table.astype(BF).astype(F32)[2 : 2 + heads]
    real = r.pad[...] > 0

    def fill_bias(i, carry):
        rows = rows_of(i, SUB)
        ids = r.buckets[rows, :]
        for h in range(heads):
            bias = lookup(jnp.broadcast_to(table[h : h + 1, :], (SUB, LANES)), ids)
            r.ds[h, rows, :] = jnp.where(real, bias, masked_score).astype(BF)
        return carry

    lax.fori_loop(0, T // SUB // 2, fill_bias, 0)
    g_o.forward()
    g_ffn[0].step(1)
    lax.fori_loop(T // SUB // 2, T // SUB, fill_bias, 0)
    g_ffn[1].step(1)
    load_x.wait()
    load_g.wait()

    g_a.finish()

    def project(b, carry):
        rows = rows_of(b, BLOCK)
        x = r.x[rows, :].astype(F32)
        n1 = (x * inverse_rms(x) * gain_attn).astype(BF)
        r.n1[rows, :] = n1
        made = dot(n1, r.wa[...].reshape(D, I3), NN).astype(BF)
        for n, out in enumerate((r.q, r.k, r.v)):
            for h in range(heads):
                out[h, rows, :] = made[:, n * I + h * HD : n * I + (h + 1) * HD]
        return carry

    lax.fori_loop(0, NB, project, 0)
    g_ffn[2].step(1)
    g_o.finish()
    s_wo.start()

    def mix(b):
        rows = slice(b * BLOCK, (b + 1) * BLOCK)
        return [dot(r.p[h, rows, :], r.v[h], NN) for h in range(heads)]

    def put_mix(b, mixed):
        rows = slice(b * BLOCK, (b + 1) * BLOCK)
        for h in range(heads):
            r.o[h, rows, :] = mixed[h]
        r.o_all[t, rows, :] = jnp.concatenate([m.astype(BF) for m in mixed], axis=1)
        s_mix[b].start()

    for b in range(NB):
        rows = slice(b * BLOCK, (b + 1) * BLOCK)
        mixed = mix(b - 1) if b > 0 else None
        weights = []
        for h in range(heads):
            scores = dot(r.q[h, rows, :], r.k[h], NT) + r.ds[h, rows, :].astype(F32)
            top = jnp.max(scores, axis=1, keepdims=True)
            e = jnp.exp(scores - top)
            weights.append((e * (1.0 / jnp.sum(e, axis=1, keepdims=True))).astype(BF))
        for h in range(heads):
            r.p[h, rows, :] = weights[h]
        if b > 0:
            put_mix(b - 1, mixed)
        if b == 0:
            g_ffn[0].step(2)
            g_ffn[1].step(2)
        if b == 1:
            g_ffn[2].step(2)
            s_wo.forward()
        if b == 2:
            g_ffn[0].step(3)
            s_mix[0].forward()
    put_mix(NB - 1, mix(NB - 1))
    g_ffn[1].step(3)
    s_mix[1].forward()
    g_ffn[2].step(3)
    s_mix[2].forward()
    s_wo.finish()
    for n in range(NT_):
        r.wo_cat[:, n * I : (n + 1) * I] = r.wo_all[n].reshape(D, I)
    g_ffn[0].step(4)
    s_mix[3].forward()
    g_ffn[1].step(4)
    for step in range(5, dp // 2 + 1):
        for g in g_ffn:
            g.step(step - 1 if g is g_ffn[2] else step)

    def halves_of(b):
        halves = [rows_of(2 * b + 1 - c, half), rows_of(2 * b + c, half)]

        def both(ref):
            return jnp.concatenate([ref[rows, :] for rows in halves], axis=0)

        def put(ref, values):
            ref[halves[0], :] = values[:half]
            ref[halves[1], :] = values[half:]

        return halves, both, put

    def feed(b):
        s_mix[b].finish()
        halves, both, put = halves_of(b)
        mixed = jnp.concatenate(
            [
                jnp.concatenate([r.o_all[n, rows, :] for n in range(NT_)], axis=1)
                for rows in halves
            ],
            axis=0,
        )
        middle = both(r.x).astype(F32) + dot(mixed, r.wo_cat[...], NT)
        r.mid[b] = middle[half:]
        n2 = (middle * inverse_rms(middle) * gain_ffn).astype(BF)
        put(r.n2, n2)
        w_gate, w_up = [w[...].reshape(D, F) for w in (r.wg, r.wu)]
        gate = dot(n2, w_gate, NN)
        up = dot(n2, w_up, NN)
        square = gate * gate
        th = jnp.tanh(gelu_scale * gate * (1.0 + gelu_cube * square))
        left = 0.5 * (1.0 + th)
        active = gate * left
        slope = left + 0.5 * gate * (1.0 - th * th) * (
            gelu_scale * (1.0 + 3.0 * gelu_cube * square)
        )
        hidden = (active * up).astype(BF)
        put(r.hidden, hidden)
        return hidden, up, active, slope

    def feed_back(b, hidden, up, active, slope):
        halves, both, put = halves_of(b)
        w_gate, w_up, w_down = [w[...].reshape(D, F) for w in (r.wg, r.wu, r.wd)]
        dhidden = dot(both(r.g), w_down, NN)
        dgate = (dhidden * up * slope).astype(BF)
        dup = (dhidden * active).astype(BF)
        put(r.dgate, dgate)
        put(r.dup, dup)
        h_mid[b].start(dot(dgate, w_gate, NT) + dot(dup, w_up, NT))
        h_out[b].start(dot(hidden, w_down, NT))

    def to_middle(b):
        rows = rows_of(2 * b + c, half)
        dn2 = h_mid[b].finish()
        dmiddle = r.g[rows, :].astype(F32) + norm_back(dn2, r.mid[b], gain_ffn)
        r.dmid[b] = dmiddle
        r.dmb[rows, :] = dmiddle.astype(BF)
        ref = r.dmb.at[rows]
        comm.send(ref, ref, partner, p_dmb[b])

    def scatter_grad(name, values):
        part = getattr(r, "part_" + name)
        part[...] = values.astype(BF).reshape(part.shape)
        sc[name].start()

    w_out = r.wo_all[t].reshape(D, I)

    def back(b):
        comm.arrived(r.dmb.at[rows_of(2 * b + 1 - c, half)], partner, p_dmb[b])
        rows = slice(b * BLOCK, (b + 1) * BLOCK)
        do = dot(r.dmb[rows, :], w_out, NN).astype(BF)
        made = []
        for h in range(heads):
            do_h = do[:, h * HD : (h + 1) * HD]
            p = r.p[h, rows, :]
            delta = jnp.sum(do_h.astype(F32) * r.o[h, rows, :], axis=1, keepdims=True)
            ds = (p.astype(F32) * (dot(do_h, r.v[h], NT) - delta)).astype(BF)
            r.ds[h, rows, :] = ds
            made.append(dot(ds, r.k[h], NN).astype(BF))
            more_k, more_v = dot(ds, r.q[h, rows, :], TN), dot(p, do_h, TN)
            if b > 0:
                more_k, more_v = r.dk[h] + more_k, r.dv[h] + more_v
            r.dk[h], r.dv[h] = more_k, more_v
        r.da[rows, 0:I] = jnp.concatenate(made, axis=1)

    for b in range(NB):
        made = feed(b)
        if b == 0:
            g_ffn[2].step(dp // 2)
        feed_back(b, *made)
        if b >= 1:
            h_mid[b - 1].middle()
    scatter_grad("d", dot(r.g[...], r.hidden[...], TN))
    h_mid[NB - 1].middle()
    scatter_grad("g", dot(r.n2[...], r.dgate[...], TN))
    to_middle(0)
    scatter_grad("u", dot(r.n2[...], r.dup[...], TN))
    for b in range(1, NB):
        to_middle(b)
        back(b - 1)
        if b == 3:
            sc["d"].middle()
    h_out[0].middle()
    back(NB - 1)
    r.da[:, I : 2 * I] = jnp.concatenate([r.dk[h].astype(BF) for h in range(heads)], axis=1)
    r.da[:, 2 * I : I3] = jnp.concatenate([r.dv[h].astype(BF) for h in range(heads)], axis=1)

    for b in range(NB):
        halves = [rows_of(2 * b + 1 - c, half), rows_of(2 * b + c, half)]
        former = jnp.concatenate([r.da[rows, :] for rows in halves], axis=0)
        h_in[b].start(dot(former, r.wa[...].reshape(D, I3), NT))
        if b >= 1:
            h_in[b - 1].middle()
    scatter_grad("a", dot(r.n1[...], r.da[...], TN))
    h_in[NB - 1].middle()
    scatter_grad("o", dot(r.dmb[...], r.o_all[t], TN))
    sc["g"].middle()
    h_out[1].middle()

    def bias_rows(i, carry):
        former, latter = [], []
        for g in range(GROUPS):
            rows = rows_of(i * GROUPS + g, GROUP)
            high, low = r.high[rows, :], r.low[rows, :]
            one, zero = jnp.ones_like(high), jnp.zeros_like(high)
            former.append(
                jnp.concatenate(
                    [jnp.where(high == BF(n), one, zero) for n in range(BUCKETS // LOW)], axis=0
                )
            )
            part = []
            for n in range(LOW):
                match = low == BF(n)
                part += [jnp.where(match, r.ds[h, rows, :], zero) for h in range(heads)]
            latter.append(jnp.concatenate(part, axis=0))
        return carry + dot(
            jnp.concatenate(former, axis=1), jnp.concatenate(latter, axis=1), NT
        )

    count = T // (GROUP * GROUPS)
    sums = lax.fori_loop(0, count // 2, bias_rows, jnp.zeros(r.bias_sum.shape, F32))
    r.bias_sum[...] = sums
    for b in range(2, NB):
        h_out[b].middle()
    sc["u"].middle()
    sc["a"].middle()
    sums = r.bias_sum[...]
    sums = lax.fori_loop(count // 2, count, bias_rows, sums)
    tall, wide = r.bias_sum.shape
    row = lax.broadcasted_iota(jnp.int32, (tall, wide), 0)
    column = lax.broadcasted_iota(jnp.int32, (tall, wide), 1)
    sums = jnp.where(row % GROUP == column % GROUP, sums, 0.0)
    sums = jnp.sum(sums.reshape(BUCKETS // LOW, GROUP, wide), axis=1)
    bucket = lax.broadcasted_iota(jnp.int32, (LANES, BUCKETS // LOW), 0)
    high = lax.broadcasted_iota(jnp.int32, (LANES, BUCKETS // LOW), 1)
    spread = jnp.where(bucket // LOW == high, 1.0, 0.0)
    spread = dot(spread.astype(BF), sums.astype(BF), NN)
    bucket = lax.broadcasted_iota(jnp.int32, (LANES, wide), 0)
    column = lax.broadcasted_iota(jnp.int32, (LANES, wide), 1)
    spread = jnp.where(bucket % LOW == column // (heads * GROUP), spread, 0.0)
    head = lax.broadcasted_iota(jnp.int32, (8, wide), 0)
    column = lax.broadcasted_iota(jnp.int32, (8, wide), 1)
    of_head = jnp.where(column // GROUP % heads == head, 1.0, 0.0)
    by_head = dot(of_head.astype(BF), spread.astype(BF), NT)
    for n in range(dp):
        moved = by_head if n == 0 else pltpu.roll(by_head, LANES - n * BR, 1)
        r.part_m[n // comm.Y, n % comm.Y] = moved
    sc["m"].start()
    sc["o"].middle()

    stores = []
    for b in range(NB):
        rows = rows_of(2 * b + c, half)
        x = r.x[rows, :].astype(F32)
        total = r.dmid[b] + norm_back(h_in[b].finish(), x, gain_attn)
        r.s_ig[b] = total.astype(BF)
        ref = r.input_grad.at[rows]
        comm.send(r.s_ig.at[b], ref, partner, p_ig[b])
        stores.append(local(r.s_ig.at[b], ref))
        stores[-1].start()
        if b == 0:
            sc["m"].middle()

    outs = {}

    def keep(name, value, out):
        ref = getattr(r, "s_" + name)
        ref[...] = value
        stores.append(local(ref, out))
        stores[-1].start()

    for n, out in zip("dgu", (r.o_d, r.o_g, r.o_u)):
        outs[n] = sc[n].finish()
        keep(n, outs[n], out)
    outs["a"] = sc["a"].finish()
    for n, name, out in zip(range(3), "qkv", (r.o_q, r.o_k, r.o_v)):
        keep(name, outs["a"][:, n * I : (n + 1) * I], out)

    def gain_grad(pairs, gain):
        total = jnp.zeros((8, R), F32)
        for weight, grad in pairs:
            product = weight.astype(F32) * grad
            total = total + dot(
                jnp.ones((8, product.shape[1]), F32), product, NT, precision=lax.Precision.HIGHEST
            )
        return total[0:1] / gain.astype(BF).astype(F32)

    r.norm[t] = jnp.zeros(r.norm.shape[1:], F32)
    r.norm[t, 0:1, 0:R] = gain_grad([(r.wa[d], outs["a"])], r.s_ga[...])
    r.norm[t, 1:2, 0:R] = gain_grad([(r.wg[d], outs["g"]), (r.wu[d], outs["u"])], r.s_gf[...])
    for n in range(1, NT_):
        ref = r.norm.at[t]
        comm.send(ref, ref, (d, (t + n) % NT_), p_norm[n])
    keep("o", sc["o"].finish(), r.o_o)
    keep("m", sc["m"].finish()[0:heads, 0:BR], r.o_m)
    for b in range(NB):
        rows = rows_of(2 * b + c, half)
        total = h_out[b].finish() + r.mid[b]
        r.s_bo[b] = total.astype(BF)
        ref = r.block_out.at[rows]
        comm.send(r.s_bo.at[b], ref, partner, p_bo[b])
        stores.append(local(r.s_bo.at[b], ref))
        stores[-1].start()
    for n in range(1, NT_):
        comm.arrived(r.norm.at[(t - n) % NT_], (d, (t + n) % NT_), p_norm[n])
    total = r.norm[0]
    for n in range(1, NT_):
        total = total + r.norm[n]
    keep("na", total[0:1, 0:R], r.o_na)
    keep("nf", total[1:2, 0:R], r.o_nf)
    for b in range(NB):
        rows = rows_of(2 * b + 1 - c, half)
        comm.arrived(r.block_out.at[rows], partner, p_bo[b])
        comm.arrived(r.input_grad.at[rows], partner, p_ig[b])
    comm.drain()
    for store in stores:
        store.wait()


def hand_over(names, pieces, *refs):
    count = len(names)
    before, after, held = [dict(zip(names, refs[n * count : (n + 1) * count])) for n in range(3)]
    wide, sems = refs[3 * count :]
    sem_at = iter(range(4 * (count + 2 * pieces)))

    def parts(name):
        rows = before[name].shape[0]
        step = rows // pieces if name in ("block_out", "input_grad") else rows
        return [slice(k, k + step) for k in range(0, rows, step)]

    jobs = []
    order = ["input_grad", "block_out"] + [n for n in names if n not in ("input_grad", "block_out")]
    for name in order:
        for rows in parts(name):
            copy = pltpu.make_async_copy(
                before[name].at[rows], held[name].at[rows], sems.at[next(sem_at)]
            )
            copy.start()
            jobs.append((name, rows, copy))
    stores = []
    for name, rows, copy in jobs:
        copy.wait()
        source = held[name]
        if name == "input_grad":
            wide[rows, :] = source[rows, :].astype(F32)
            source = wide
        stores.append(
            pltpu.make_async_copy(source.at[rows], after[name].at[rows], sems.at[next(sem_at)])
        )
        stores[-1].start()
    for store in stores:
        store.wait()


def per_device(
    sizes,
    tokens,
    cotangent,
    w_query,
    w_key,
    w_value,
    w_out,
    w_gate,
    w_up,
    w_down,
    norm_attn,
    norm_ffn,
    bias_table,
    buckets,
    padding,
):
    T, D = tokens.shape
    R, I = w_query.shape
    F = w_gate.shape[1]
    BR, heads = bias_table.shape
    HD = I // heads
    Z, Y, X = sizes
    dp, tensor = Z * Y, 2 * X
    NB, half = T // BLOCK, BLOCK // 2
    S, V = jax.ShapeDtypeStruct, pltpu.VMEM
    inputs = dict(
        x_in=tokens,
        g_in=cotangent,
        wq_in=w_query,
        wk_in=w_key,
        wv_in=w_value,
        wo_in=w_out.T,
        wg_in=w_gate,
        wu_in=w_up,
        wd_in=w_down.T,
        ga_in=norm_attn.reshape(1, R),
        gf_in=norm_ffn.reshape(1, R),
        bt_in=bias_table.T,
        bucket_in=buckets,
        pad_in=padding,
    )
    outputs = dict(
        block_out=S((T, D), BF),
        input_grad=S((T, D), BF),
        o_q=S((R, I), F32),
        o_k=S((R, I), F32),
        o_v=S((R, I), F32),
        o_o=S((R, I), F32),
        o_g=S((R, F), F32),
        o_u=S((R, F), F32),
        o_d=S((R, F), F32),
        o_na=S((1, R), F32),
        o_nf=S((1, R), F32),
        o_m=S((heads, BR), F32),
    )
    scratch = dict(
        s_attn=V((4, R, I), F32),
        s_ffn=V((3, R, F), F32),
        s_ga=V((1, R), F32),
        s_gf=V((1, R), F32),
        s_bt=V((heads, BR), F32),
        x=V((T, D), BF),
        g=V((T, D), BF),
        buckets=V((T, T), jnp.int32),
        pad=V((1, T), jnp.int32),
        misc=V((dp, 8, LANES), F32),
        wa=V((dp, R, 3 * I), BF),
        high=V((T, T), BF),
        low=V((T, T), BF),
        wo_all=V((tensor, dp, R, I), BF),
        wo_cat=V((D, tensor * I), BF),
        wg=V((dp, R, F), BF),
        wu=V((dp, R, F), BF),
        wd=V((dp, R, F), BF),
        n1=V((T, D), BF),
        q=V((heads, T, HD), BF),
        k=V((heads, T, HD), BF),
        v=V((heads, T, HD), BF),
        p=V((heads, T, T), BF),
        o=V((heads, T, HD), F32),
        o_all=V((tensor, T, I), BF),
        mid=V((NB, half, D), F32),
        n2=V((T, D), BF),
        hidden=V((T, F), BF),
        dgate=V((T, F), BF),
        dup=V((T, F), BF),
        m_away=V((NB, half, D), BF),
        m_kept=V((NB, half, D), F32),
        m_near=V((NB, half, D), BF),
        m_far=V((X, NB, half, D), BF),
        f_away=V((NB, half, D), BF),
        f_kept=V((NB, half, D), F32),
        f_near=V((NB, half, D), BF),
        f_far=V((X, NB, half, D), BF),
        dmid=V((NB, half, D), F32),
        dmb=V((T, D), BF),
        i_away=V((NB, half, D), BF),
        i_kept=V((NB, half, D), F32),
        i_near=V((NB, half, D), BF),
        i_far=V((X, NB, half, D), BF),
        dk=V((heads, T, HD), F32),
        dv=V((heads, T, HD), F32),
        da=V((T, 3 * I), BF),
        ds=V((heads, T, T), BF),
        bias_sum=V((BUCKETS // LOW * GROUP, LOW * heads * GROUP), F32),
        s_bo=V((NB, half, D), BF),
        s_ig=V((NB, half, D), BF),
        norm=V((tensor, 8, LANES), F32),
        s_m=V((heads, BR), F32),
        s_na=V((1, R), F32),
        s_nf=V((1, R), F32),
    )
    widths = dict(a=3 * I, o=I, g=F, u=F, d=F)
    for n, width in widths.items():
        scratch["part_" + n] = V((Z, Y, R, width), BF)
        scratch["fy_" + n] = V((Y - 1, Z, R, width), BF)
        scratch["mine_" + n] = V((Z, R, width), BF)
        scratch["fz_" + n] = V((Z - 1, R, width), BF)
    for n, width in dict(q=I, k=I, v=I, o=I, g=F, u=F, d=F).items():
        scratch["s_" + n] = V((R, width), F32)
    scratch["part_m"] = V((Z, Y, 8, LANES), F32)
    scratch["fy_m"] = V((Y - 1, Z, 8, LANES), F32)
    scratch["mine_m"] = V((Z, 8, LANES), F32)
    scratch["fz_m"] = V((Z - 1, 8, LANES), F32)
    count = 3 * (Z - 1 + Z * (Y - 1)) + 3 * (dp - 1) + (1 + NB) * (2 * X - 1)
    count += 3 * NB * X + 3 * NB + tensor - 1 + 6 * (Y + Z - 2)
    scratch["local_sems"] = pltpu.SemaphoreType.DMA((14 + 2 * NB + 10,))
    scratch["sems"] = pltpu.SemaphoreType.DMA((2 * count,))
    names = [*inputs, *outputs, *scratch]
    made = pl.pallas_call(
        functools.partial(layer_kernel, sizes, heads, names),
        out_shape=list(outputs.values()),
        in_specs=[pl.BlockSpec(memory_space=pl.ANY)] * len(inputs),
        out_specs=[pl.BlockSpec(memory_space=pl.ANY)] * len(outputs),
        scratch_shapes=list(scratch.values()),
        compiler_params=pltpu.CompilerParams(
            collective_id=0, has_side_effects=True, vmem_limit_bytes=62 << 20
        ),
        name="layer",
    )(*inputs.values())
    final = {**outputs, "input_grad": S((T, D), F32)}
    pieces = 4
    made = pl.pallas_call(
        functools.partial(hand_over, list(outputs), pieces),
        out_shape=list(final.values()),
        in_specs=[pl.BlockSpec(memory_space=pl.ANY)] * len(outputs),
        out_specs=[pl.BlockSpec(memory_space=pl.ANY)] * len(outputs),
        scratch_shapes=[V(o.shape, o.dtype) for o in outputs.values()]
        + [V((T, D), F32), pltpu.SemaphoreType.DMA((4 * (len(outputs) + 2 * pieces),))],
        name="hand_over",
    )(*made)
    out = dict(zip(outputs, made))
    return (
        out["block_out"],
        out["input_grad"],
        out["o_q"],
        out["o_k"],
        out["o_v"],
        out["o_o"].T,
        out["o_g"],
        out["o_u"],
        out["o_d"].T,
        out["o_na"].reshape(R),
        out["o_nf"].reshape(R),
        out["o_m"].T,
    )


def solution(mesh):
    shards, halves = mesh.shape["dp"], mesh.shape["tensor"]
    X = halves // 2
    Y = X if shards % X == 0 else 1
    sizes = (shards // Y, Y, X)
    in_specs = (
        P("dp", None),
        P("dp", None),
        P("dp", "tensor"),
        P("dp", "tensor"),
        P("dp", "tensor"),
        P("tensor", "dp"),
        P("dp", "tensor"),
        P("dp", "tensor"),
        P("tensor", "dp"),
        P("dp"),
        P("dp"),
        P("dp", "tensor"),
        P(),
        P("dp", None),
    )
    out_specs = (
        P("dp", None),
        P("dp", None),
        P("dp", "tensor"),
        P("dp", "tensor"),
        P("dp", "tensor"),
        P("tensor", "dp"),
        P("dp", "tensor"),
        P("dp", "tensor"),
        P("tensor", "dp"),
        P("dp"),
        P("dp"),
        P("dp", "tensor"),
    )
    return jax.shard_map(
        functools.partial(per_device, sizes),
        mesh=mesh,
        in_specs=in_specs,
        out_specs=out_specs,
        check_vma=False,
    )
```
